256 devices in a mesh: section: 4 (over z_lo), tensor: 8 (over x, z_hi), dp: 8 (over y, core).
Axes of the slice: x: 4, y: 4, z: 8 (z_hi: 2, z_lo: 4; z = z_hi * 4 + z_lo), core: 2. Of those that a mesh axis runs over, the one named last changes fastest.
Arguments:
- hidden_in: bfloat16 [16, 64, 4096], P('dp', None, 'tensor'), may hold values from -6 to 6
- lengths: int32 [16], P('dp'), may hold values from 16 to 64
- gains: bfloat16 [4, 4096], P('section', 'tensor'), may hold values from 0.25 to 1.75
- w_query: bfloat16 [4, 4096, 4096], P('section', None, 'tensor'), may hold values from -0.09375 to 0.09375
- w_keyval: bfloat16 [4, 4096, 8, 256], P('section', None, 'tensor'), may hold values from -0.09375 to 0.09375
- w_out: bfloat16 [4, 4096, 4096], P('section', 'tensor'), may hold values from -0.09375 to 0.09375
- grad_out: bfloat16 [16, 64, 4096], P('dp', None, 'tensor'), may hold values from -6 to 6
Outputs:
- grad_query: float32 [4, 4096, 4096], P('section', 'dp', 'tensor')
- grad_keyval: float32 [4, 4096, 8, 256], P('section', 'dp', 'tensor')
- grad_outproj: float32 [4, 4096, 4096], P('section', 'tensor', 'dp')
- grad_gain: float32 [4, 4096], P('section', ('tensor', 'dp'))
The draws below stay inside these ranges and needn't reach their ends.
Inputs may be any that keep to these rules, and one draw needn't show every extreme that they name: `lengths`: A row's keys at positions at or beyond its length are padding.
All inputs are finite; a program needn't handle non-finite values.
Results may differ from the reference program's by a relative error of at most 0.035.
Values may be sent and summed in bfloat16 or wider, within the bound.
No kernel may reach another device: no remote copies, remote signals or barrier semaphores. Data moves between devices by JAX's collectives and lax.ppermute only.
A program may use at most 128 MiB of HBM per device.

```python
import jax
import jax.numpy as jnp
from jax import lax

D = 4096
HEADS = 32
KV_HEADS = 8
HEAD_DIM = 128
LEN = 64
MICRO = 2
BATCH = 16
N_SECTION = 4
N_DP = 8


def touch_ends(array, own_key, smallest, top_value):
    longest = array.shape.index(max(array.shape))
    spots = []
    for shift in (0, 1):
        where = [jax.random.randint(jax.random.fold_in(own_key, axis), (), 0, length) for axis, length in enumerate(array.shape)]
        where[longest] = (where[longest] + shift) % array.shape[longest]
        spots.append(tuple(where))
    return array.at[spots[0]].set(smallest).at[spots[1]].set(top_value)


def block_levels(rng, extent, cuts, least, high):
    def one(axis_at, shards_of):
        heights = jax.random.uniform(jax.random.fold_in(jax.random.fold_in(rng, 6), axis_at), (shards_of,), jnp.float32, least / len(cuts), high / len(cuts))
        return jnp.repeat(jnp.exp(heights), extent[axis_at] // shards_of).reshape((-1,) + (1,) * (len(extent) - axis_at - 1))

    gain = one(*cuts[0])
    for cut in cuts[1:]:
        gain = gain * one(*cut)
    return gain


def normal_values(key, extent, deviation, bound, cuts=(), dtype=jnp.bfloat16):
    gain = block_levels(key, extent, cuts, -0.22, 0.18) if cuts else 1.0
    values = jax.random.normal(key, extent, jnp.float32) * deviation * gain
    return jnp.minimum(jnp.maximum(values, -bound), bound).astype(dtype)


def setup_inputs(seed: int = 0) -> dict:
    key_list = jax.random.split(jax.random.key(seed), 8)
    hidden_in = normal_values(key_list[0], (BATCH, LEN, D), 1.0, 6.0, ((0, 8), (2, 8)))
    lengths = touch_ends(jax.random.randint(key_list[1], (BATCH,), LEN // 4, LEN + 1), jax.random.fold_in(key_list[1], 1), LEN // 4, LEN).astype(jnp.int32)
    gains = jnp.clip(1.0 + 0.15 * jax.random.normal(key_list[2], (N_SECTION, D), jnp.float32), 0.25, 1.75).astype(jnp.bfloat16)
    w_query = normal_values(key_list[3], (N_SECTION, D, HEADS * HEAD_DIM), D ** -0.5, 0.09375, ((0, 4), (2, 8)))
    w_keyval = normal_values(key_list[4], (N_SECTION, D, KV_HEADS, 2 * HEAD_DIM), D ** -0.5, 0.09375, ((0, 4), (2, 8)))
    w_out = normal_values(key_list[5], (N_SECTION, HEADS * HEAD_DIM, D), (HEADS * HEAD_DIM) ** -0.5, 0.09375, ((0, 4), (1, 8)))
    grad_out = normal_values(key_list[6], (BATCH, LEN, D), 1.0, 6.0, ((0, 8), (2, 8)))
    return {"hidden_in": hidden_in, "lengths": lengths, "gains": gains, "w_query": w_query, "w_keyval": w_keyval, "w_out": w_out, "grad_out": grad_out}


EPS = 1e-05
NEG = -1e+30

def settle(operand):
    return lax.optimization_barrier(operand.astype(jnp.bfloat16)).astype(jnp.float32)

def attend(queries, keyval, length):
    row_count = queries.shape[0]
    group_size = HEADS // KV_HEADS
    query_heads = queries.astype(jnp.float32).reshape(row_count, KV_HEADS, group_size, HEAD_DIM)
    pairs = keyval.astype(jnp.float32).reshape(row_count, KV_HEADS, 2, HEAD_DIM)
    scores = jnp.einsum('ighd,jgd->ghij', query_heads, pairs[:, :, 0]) * HEAD_DIM ** (-0.5)
    position = jnp.arange(row_count)
    allowed = (position[None, :] <= position[:, None]) & (position[None, :] < length)
    scores = jnp.where(allowed, scores, NEG)
    highest = lax.optimization_barrier(jnp.max(scores, -1, keepdims=True))
    raised = jnp.exp(scores - highest)
    attn_weights = raised / lax.optimization_barrier(jnp.sum(raised, -1, keepdims=True))
    head_mix = jnp.einsum('ghij,jgd->ighd', settle(attn_weights), pairs[:, :, 1])
    return (head_mix.reshape(row_count, -1).astype(jnp.bfloat16), attn_weights)

def attend_back(queries, keyval, attn_weights, mix_grad):
    row_count = queries.shape[0]
    group_size = HEADS // KV_HEADS
    query_heads = queries.astype(jnp.float32).reshape(row_count, KV_HEADS, group_size, HEAD_DIM)
    pairs = keyval.astype(jnp.float32).reshape(row_count, KV_HEADS, 2, HEAD_DIM)
    grad_heads = mix_grad.astype(jnp.float32).reshape(row_count, KV_HEADS, group_size, HEAD_DIM)
    value_grad = jnp.einsum('ghij,ighd->jgd', settle(attn_weights), grad_heads).astype(jnp.bfloat16)
    weight_grad = jnp.einsum('ighd,jgd->ghij', grad_heads, pairs[:, :, 1])
    score_grad = attn_weights * (weight_grad - lax.optimization_barrier(jnp.sum(weight_grad * attn_weights, -1, keepdims=True))) * HEAD_DIM ** (-0.5)
    score_grad = settle(score_grad)
    query_grad = jnp.einsum('ghij,jgd->ighd', score_grad, pairs[:, :, 0]).reshape(row_count, -1).astype(jnp.bfloat16)
    key_grad = jnp.einsum('ghij,ighd->jgd', score_grad, query_heads).astype(jnp.bfloat16)
    return (query_grad, jnp.stack([key_grad, value_grad], 2).reshape(row_count, -1))

def layer_forward(current, length, gain_row, query_weight, pair_weight, out_weight):
    current_wide = current.astype(jnp.float32)
    scale_row = lax.rsqrt(lax.optimization_barrier(jnp.sum(current_wide * current_wide, -1)) / D + EPS)
    normed = (current_wide * scale_row[:, None] * gain_row).astype(jnp.bfloat16)
    queries = jnp.dot(normed, query_weight, preferred_element_type=jnp.float32).astype(jnp.bfloat16)
    keyval = jnp.dot(normed, pair_weight, preferred_element_type=jnp.float32).astype(jnp.bfloat16)
    head_mix, attn_weights = attend(queries, keyval, length)
    result = (current_wide + jnp.dot(head_mix, out_weight, preferred_element_type=jnp.float32)).astype(jnp.bfloat16)
    return (result, (scale_row, normed, queries, keyval, head_mix, attn_weights))

def layer_backward(current, gain_row, query_weight, pair_weight, out_weight, kept, out_grad):
    scale_row, normed, queries, keyval, head_mix, attn_weights = kept
    mix_grad = jnp.dot(out_grad, out_weight.T, preferred_element_type=jnp.float32).astype(jnp.bfloat16)
    out_term = jnp.dot(head_mix.T, out_grad, preferred_element_type=jnp.float32)
    query_grad, pair_grad = attend_back(queries, keyval, attn_weights, mix_grad)
    query_term = jnp.dot(normed.T, query_grad, preferred_element_type=jnp.float32)
    pair_term = jnp.dot(normed.T, pair_grad, preferred_element_type=jnp.float32)
    normed_grad = jnp.dot(query_grad, query_weight.T, preferred_element_type=jnp.float32) + jnp.dot(pair_grad, pair_weight.T, preferred_element_type=jnp.float32)
    current_wide = current.astype(jnp.float32)
    gain_term = lax.optimization_barrier(jnp.sum(normed_grad * current_wide * scale_row[:, None], 0))
    correction = lax.optimization_barrier(jnp.sum(normed_grad * gain_row * current_wide, -1))
    input_grad = (out_grad.astype(jnp.float32) + scale_row[:, None] * gain_row * normed_grad - current_wide * (scale_row ** 3 / D)[:, None] * correction[:, None]).astype(jnp.bfloat16)
    return (input_grad, (query_term, pair_term, out_term, gain_term))

def reference(hidden_in, lengths, gains, w_query, w_keyval, w_out, grad_out):
    pair_weights = w_keyval.reshape(N_SECTION, D, -1)
    rows_all = hidden_in.reshape(N_DP, MICRO, LEN, D)
    lens_all = lengths.reshape(N_DP, MICRO)
    cots_all = grad_out.reshape(N_DP, MICRO, LEN, D)
    shapes = [(D, HEADS * HEAD_DIM), (D, KV_HEADS * 2 * HEAD_DIM), (HEADS * HEAD_DIM, D), (D,)]

    def replica(totals, replica_item):
        rows_here, lens_here, cots_here = replica_item
        section_sums = [tuple((jnp.zeros(shape_one, jnp.float32) for shape_one in shapes)) for section in range(N_SECTION)]
        for batch_row in range(MICRO):
            current = rows_here[batch_row]
            length = lens_here[batch_row]
            inputs = []
            kept_all = []
            for section in range(N_SECTION):
                inputs.append(current)
                current, kept = layer_forward(current, length, gains[section], w_query[section], pair_weights[section], w_out[section])
                kept_all.append(kept)
            out_grad = cots_here[batch_row]
            for section in reversed(range(N_SECTION)):
                out_grad, terms = layer_backward(inputs[section], gains[section], w_query[section], pair_weights[section], w_out[section], kept_all[section], out_grad)
                section_sums[section] = tuple((former + latter for former, latter in zip(section_sums[section], terms)))
        new_totals = tuple((total + jnp.stack([section_sums[section][member] for section in range(N_SECTION)]) for member, total in enumerate(totals)))
        return (new_totals, None)
    start = tuple((jnp.zeros((N_SECTION,) + shape_one, jnp.float32) for shape_one in shapes))
    totals, unused = lax.scan(replica, start, (rows_all, lens_all, cots_all))
    return (totals[0], totals[1].reshape(N_SECTION, D, KV_HEADS, 2 * HEAD_DIM), totals[2], totals[3])
```

```python
import jax
import jax.numpy as jnp
from jax import lax
from jax.sharding import Mesh, PartitionSpec as P

HEAD_DIM = 128
EPS = 1e-05
NEG = -1e30
F32 = jnp.float32
BF16 = jnp.bfloat16
SECTIONS, XS, HALVES = 4, 4, 2


def dot(former, latter, dims):
    return lax.dot_general(former, latter, (dims, ((), ())), preferred_element_type=F32)


def place(section, x, half):
    return (section * XS + x) * HALVES + half


def gather_x(block):
    spread = jnp.broadcast_to(block[None], (XS,) + block.shape)
    parts = lax.all_to_all(spread, "x", 0, 0)
    return jnp.concatenate([parts[j] for j in range(XS)], axis=-1)


def scatter_x(wide):
    width = wide.shape[1] // XS
    parts = jnp.stack([wide[:, j * width : (j + 1) * width] for j in range(XS)])
    return jnp.sum(lax.all_to_all(parts, "x", 0, 0).astype(F32), 0)


def hop(block, source, target):
    total = None
    for cross in range(HALVES):
        route = [
            (place(source, x, half), place(target, x, half ^ cross))
            for x in range(XS)
            for half in range(HALVES)
        ]
        got = lax.ppermute(block, ("s", "x", "zh"), route).astype(F32)
        total = got if total is None else total + got
    return total.astype(BF16)


def pair_up(block):
    route = [
        (place(s, x, half), place(s, x, 1 - half))
        for s in range(SECTIONS)
        for x in range(XS)
        for half in range(HALVES)
    ]
    other = lax.ppermute(block, ("s", "x", "zh"), route)
    first = lax.axis_index("zh") == 0
    return jnp.concatenate([jnp.where(first, block, other), jnp.where(first, other, block)], -1)


def pick(items, station):
    chosen = items[0]
    for s in range(1, SECTIONS):
        chosen = jnp.where(station == s, items[s], chosen)
    return chosen


def attend(queries, keyval, lengths, rows, length):
    group = queries.shape[1] // HEAD_DIM
    q = queries.reshape(rows, length, group, HEAD_DIM)
    keys = keyval[:, :HEAD_DIM].reshape(rows, length, HEAD_DIM)
    values = keyval[:, HEAD_DIM:].reshape(rows, length, HEAD_DIM)
    scores = jnp.einsum("rigd,rjd->rgij", q, keys, preferred_element_type=F32) * HEAD_DIM ** (-0.5)
    position = jnp.arange(length)
    allowed = (position[None, None, :] <= position[None, :, None]) & (
        position[None, None, :] < lengths[:, None, None]
    )
    scores = jnp.where(allowed[:, None], scores, NEG)
    raised = jnp.exp(scores - jnp.max(scores, -1, keepdims=True))
    weights = raised / jnp.sum(raised, -1, keepdims=True)
    mix = jnp.einsum("rgij,rjd->rigd", weights.astype(BF16), values, preferred_element_type=F32)
    return mix.reshape(rows * length, -1).astype(BF16), weights


def attend_back(queries, keyval, weights, mix_grad, rows, length):
    group = queries.shape[1] // HEAD_DIM
    q = queries.reshape(rows, length, group, HEAD_DIM)
    keys = keyval[:, :HEAD_DIM].reshape(rows, length, HEAD_DIM)
    values = keyval[:, HEAD_DIM:].reshape(rows, length, HEAD_DIM)
    grads = mix_grad.reshape(rows, length, group, HEAD_DIM)
    value_grad = jnp.einsum("rgij,rigd->rjd", weights.astype(BF16), grads, preferred_element_type=F32)
    weight_grad = jnp.einsum("rigd,rjd->rgij", grads, values, preferred_element_type=F32)
    score_grad = (
        weights * (weight_grad - jnp.sum(weight_grad * weights, -1, keepdims=True)) * HEAD_DIM ** (-0.5)
    ).astype(BF16)
    query_grad = jnp.einsum("rgij,rjd->rigd", score_grad, keys, preferred_element_type=F32)
    key_grad = jnp.einsum("rgij,rigd->rjd", score_grad, q, preferred_element_type=F32)
    pair_grad = jnp.concatenate([key_grad, value_grad], -1).reshape(rows * length, -1)
    return query_grad.reshape(rows * length, -1).astype(BF16), pair_grad.astype(BF16)


def shards(hidden_in, lengths, gains, w_query, w_keyval, w_out, grad_out):
    station = lax.axis_index("s")
    x = lax.axis_index("x")
    rows, length, shard = hidden_in.shape
    tokens = rows * length
    query_weight = w_query[0]
    width = query_weight.shape[0]
    pair_weight = w_keyval[0].reshape(width, -1)
    out_weight = w_out[0]
    block_width = width // XS

    start = jnp.where(
        station == 0, hidden_in.reshape(tokens, shard), grad_out.reshape(tokens, shard)
    )
    start = jnp.concatenate([start, jnp.broadcast_to(gains, (16, shard))], 0)
    start_block = pair_up(start)
    start_full = gather_x(start_block)
    gain_row = start_full[tokens].astype(F32)
    block = start_block[:tokens]
    full = start_full[:tokens]

    def own(wide):
        return lax.dynamic_slice_in_dim(wide, x * block_width, block_width, 1)

    kept = []
    for step in range(SECTIONS):
        if step:
            full = gather_x(block)
        wide = full.astype(F32)
        scale = lax.rsqrt(jnp.sum(wide * wide, -1, keepdims=True) / width + EPS)
        normed = (wide * scale * gain_row).astype(BF16)
        queries = dot(normed, query_weight, ((1,), (0,))).astype(BF16)
        keyval = dot(normed, pair_weight, ((1,), (0,))).astype(BF16)
        mix, weights = attend(queries, keyval, lengths, rows, length)
        kept.append((full, scale, normed, queries, keyval, mix, weights))
        if step + 1 < SECTIONS:
            branch = scatter_x(dot(mix, out_weight, ((1,), (0,))).astype(BF16))
            block = hop((0.5 * block.astype(F32) + branch).astype(BF16), step, step + 1)

    block = start_block[:tokens]
    full_grad = start_full[:tokens]
    found = [None] * SECTIONS
    for step in reversed(range(SECTIONS)):
        if step + 1 < SECTIONS:
            full_grad = gather_x(block)
        full, scale, normed, queries, keyval, mix, weights = kept[step]
        wide = full.astype(F32)
        mix_grad = dot(full_grad, out_weight, ((1,), (1,))).astype(BF16)
        query_grad, pair_grad = attend_back(queries, keyval, weights, mix_grad, rows, length)
        normed_grad = dot(query_grad, query_weight, ((1,), (1,))) + dot(
            pair_grad, pair_weight, ((1,), (1,))
        )
        gain_part = jnp.sum(normed_grad * wide * scale, 0)
        found[step] = (normed, full_grad, query_grad, pair_grad, mix, gain_part)
        if step:
            correction = jnp.sum(normed_grad * gain_row * wide, -1, keepdims=True)
            change = scale * gain_row * normed_grad - wide * (scale**3 / width) * correction
            branch = scatter_x(change.astype(BF16))
            block = hop((0.5 * block.astype(F32) + branch).astype(BF16), step, step - 1)

    normed, full_grad, query_grad, pair_grad, mix, gain_part = [
        pick(items, station) for items in zip(*found)
    ]
    dp = 8
    small = width // dp
    cut = lambda wide: wide.reshape(tokens, dp, small).transpose(1, 0, 2)
    spread = lambda narrow: jnp.broadcast_to(narrow[None], (dp,) + narrow.shape)
    send = jnp.concatenate(
        [cut(normed), cut(full_grad), spread(query_grad), spread(pair_grad), spread(mix)], -1
    )
    got = lax.all_to_all(send, ("y", "core"), 0, 0).reshape(dp * tokens, -1)
    edges = [0]
    for piece in (small, small, query_grad.shape[1], pair_grad.shape[1], mix.shape[1]):
        edges.append(edges[-1] + piece)
    normed, full_grad, query_grad, pair_grad, mix = [
        got[:, a:b] for a, b in zip(edges[:-1], edges[1:])
    ]
    grad_query = dot(normed, query_grad, ((0,), (0,)))
    grad_pair = dot(normed, pair_grad, ((0,), (0,)))
    grad_out_weight = dot(mix, full_grad, ((0,), (0,)))

    pieces = gain_part.reshape(8, dp, -1)
    pieces = lax.all_to_all(pieces.transpose(1, 0, 2), ("y", "core"), 0, 0)
    pieces = jnp.sum(pieces, 0)
    pieces = lax.all_to_all(pieces, ("x", "zh"), 0, 0)
    gain_grad = jnp.sum(pieces, 0)
    return (
        grad_query[None],
        grad_pair.reshape(1, small, 1, -1),
        grad_out_weight[None],
        gain_grad[None],
    )


def solution(mesh):
    grid = Mesh(mesh.devices.reshape(SECTIONS, XS, HALVES, 4, 2), ("s", "x", "zh", "y", "core"))
    section, tensor, dp = "s", ("x", "zh"), ("y", "core")
    in_specs = (
        P(dp, None, tensor),
        P(dp),
        P(section, tensor),
        P(section, None, tensor),
        P(section, None, tensor, None),
        P(section, tensor, None),
        P(dp, None, tensor),
    )
    out_specs = (
        P(section, dp, tensor),
        P(section, dp, tensor, None),
        P(section, tensor, dp),
        P(section, tensor + dp),
    )
    return jax.shard_map(shards, mesh=grid, in_specs=in_specs, out_specs=out_specs, check_vma=False)
```

```python
import functools

import jax
import jax.numpy as jnp
from jax import lax
from jax.experimental import pallas as pl
from jax.experimental.pallas import tpu as pltpu
from jax.sharding import Mesh, PartitionSpec as P

HEAD_DIM = 128
EPS = 1e-05
NEG = -1e30
F32 = jnp.float32
BF16 = jnp.bfloat16
SECTIONS, XS, HALVES, DP = 4, 4, 2, 8
VMEM = pl.BlockSpec(memory_space=pltpu.VMEM)
SMEM = pl.BlockSpec(memory_space=pltpu.SMEM)
HBM = pl.BlockSpec(memory_space=pl.ANY)


def dot(former, latter, dims=((1,), (0,))):
    return lax.dot_general(former, latter, (dims, ((), ())), preferred_element_type=F32)


def copies(pairs, sems):
    return [pltpu.make_async_copy(a, b, sems.at[i]) for i, (a, b) in enumerate(pairs)]


def heads_down(wide, row, length):
    part = wide[row * length : (row + 1) * length, :]
    return jnp.concatenate(
        [part[:, a : a + HEAD_DIM] for a in range(0, part.shape[1], HEAD_DIM)], axis=0
    )


def heads_across(tall, length):
    return jnp.concatenate(
        [tall[a : a + length] for a in range(0, tall.shape[0], length)], axis=1
    )


def forward_kernel(
    rows, length, project, lens, parts, gain, wq, wkv, wo, *rest
):
    if project:
        send, scale_out, q_out, kv_out, mix_out, attn_out, wq_v, wkv_v, wo_v, sems = rest
    else:
        scale_out, q_out, kv_out, mix_out, attn_out, wq_v, wkv_v, sems = rest
    block = parts.shape[2]
    width = XS * block
    pairs = []
    for j in range(XS):
        span = pl.ds(j * block, block)
        pairs.append((wq.at[span], wq_v.at[span]))
        pairs.append((wkv.at[span], wkv_v.at[span]))
    if project:
        for j in range(XS):
            span = pl.ds(j * block, block)
            pairs.append((wo.at[:, span], wo_v.at[:, span]))
    moves = copies(pairs, sems)
    for move in moves:
        move.start()
    total = jnp.zeros((parts.shape[1], 1), F32)
    for j in range(XS):
        h = parts[j].astype(F32)
        total = total + jnp.sum(h * h, -1, keepdims=True)
    scale = lax.rsqrt(total / width + EPS)
    scale_out[...] = scale
    q = jnp.zeros(q_out.shape, F32)
    kv = jnp.zeros(kv_out.shape, F32)
    for j in range(XS):
        span = slice(j * block, (j + 1) * block)
        normed = (parts[j].astype(F32) * scale * gain[:, span].astype(F32)).astype(BF16)
        moves[2 * j].wait()
        q = q + dot(normed, wq_v[span, :])
        moves[2 * j + 1].wait()
        kv = kv + dot(normed, wkv_v[span, :])
    q = q.astype(BF16)
    kv = kv.astype(BF16)
    q_out[...] = q
    kv_out[...] = kv
    tall = q.shape[1] // HEAD_DIM * length
    at = lax.broadcasted_iota(jnp.int32, (tall, length), 0) % length
    key_at = lax.broadcasted_iota(jnp.int32, (tall, length), 1)
    mixes = []
    for row in range(rows):
        here = slice(row * length, (row + 1) * length)
        keys, values = kv[here, :HEAD_DIM], kv[here, HEAD_DIM:]
        scores = dot(heads_down(q, row, length), keys, ((1,), (1,))) * HEAD_DIM ** (-0.5)
        scores = jnp.where((key_at <= at) & (key_at < lens[row]), scores, NEG)
        raised = jnp.exp(scores - jnp.max(scores, -1, keepdims=True))
        attn = raised / jnp.sum(raised, -1, keepdims=True)
        attn_out[row] = attn
        mixes.append(heads_across(dot(attn.astype(BF16), values).astype(BF16), length))
    mix = jnp.concatenate(mixes, axis=0)
    mix_out[...] = mix
    if project:
        for j in range(XS):
            moves[2 * XS + j].wait()
            send[j] = dot(mix, wo_v[:, j * block : (j + 1) * block]).astype(BF16)


def backward_kernel(
    rows, length, onward, grads, parts, gain, scale_in, q_in, kv_in, attn_in, wq, wkv, wo, *rest
):
    if onward:
        send, qg_out, pg_out, gain_out, wq_v, wkv_v, wo_v, sems = rest
    else:
        qg_out, pg_out, gain_out, wq_v, wkv_v, wo_v, sems = rest
    block = parts.shape[2]
    width = XS * block
    pairs = []
    for j in range(XS):
        span = pl.ds(j * block, block)
        pairs.append((wo.at[:, span], wo_v.at[:, span]))
    for j in range(XS):
        span = pl.ds(j * block, block)
        pairs.append((wq.at[span], wq_v.at[span]))
        pairs.append((wkv.at[span], wkv_v.at[span]))
    moves = copies(pairs, sems)
    for move in moves:
        move.start()
    mix_grad = jnp.zeros(q_in.shape, F32)
    for j in range(XS):
        moves[j].wait()
        mix_grad = mix_grad + dot(grads[j], wo_v[:, j * block : (j + 1) * block], ((1,), (1,)))
    mix_grad = mix_grad.astype(BF16)
    q = q_in[...]
    kv = kv_in[...]
    query_grads, pair_grads = [], []
    for row in range(rows):
        here = slice(row * length, (row + 1) * length)
        keys, values = kv[here, :HEAD_DIM], kv[here, HEAD_DIM:]
        attn = attn_in[row]
        mixed = heads_down(mix_grad, row, length)
        value_grad = dot(attn.astype(BF16), mixed, ((0,), (0,)))
        weight_grad = dot(mixed, values, ((1,), (1,)))
        score_grad = attn * (weight_grad - jnp.sum(weight_grad * attn, -1, keepdims=True))
        score_grad = (score_grad * HEAD_DIM ** (-0.5)).astype(BF16)
        query_grads.append(heads_across(dot(score_grad, keys).astype(BF16), length))
        key_grad = dot(score_grad, heads_down(q, row, length), ((0,), (0,)))
        pair_grads.append(jnp.concatenate([key_grad, value_grad], axis=1).astype(BF16))
    query_grad = jnp.concatenate(query_grads, axis=0)
    pair_grad = jnp.concatenate(pair_grads, axis=0)
    qg_out[...] = query_grad
    pg_out[...] = pair_grad
    scale = scale_in[...]
    if onward:
        correction = jnp.sum(query_grad.astype(F32) * q.astype(F32), -1, keepdims=True)
        correction += jnp.sum(pair_grad.astype(F32) * kv.astype(F32), -1, keepdims=True)
        pull = scale * scale / width * correction
    for j in range(XS):
        span = slice(j * block, (j + 1) * block)
        moves[XS + 2 * j].wait()
        moves[XS + 2 * j + 1].wait()
        normed_grad = dot(query_grad, wq_v[span, :], ((1,), (1,))) + dot(
            pair_grad, wkv_v[span, :], ((1,), (1,))
        )
        h = parts[j].astype(F32)
        scaled = normed_grad * scale
        gain_out[:, span] = jnp.sum(scaled * h, 0, keepdims=True)
        if onward:
            send[j] = (scaled * gain[:, span].astype(F32) - h * pull).astype(BF16)


def call(kernel, outs, scratch, sems, flops, args):
    specs = [SMEM if a.dtype == jnp.int32 else HBM if a.size > 2**20 - 1 else VMEM for a in args]
    return pl.pallas_call(
        kernel,
        out_shape=outs,
        in_specs=specs,
        out_specs=[VMEM] * len(outs),
        scratch_shapes=scratch + [pltpu.SemaphoreType.DMA((sems,))],
        compiler_params=pltpu.CompilerParams(vmem_limit_bytes=32 * 2**20),
        cost_estimate=pl.CostEstimate(flops=flops, bytes_accessed=12 * 2**20, transcendentals=2**16),
    )(*args)


def place(section, x, half):
    return (section * XS + x) * HALVES + half


def gather_x(spread):
    return lax.all_to_all(spread, "x", 0, 0)


def scatter_x(parts):
    return jnp.sum(lax.all_to_all(parts, "x", 0, 0).astype(F32), 0)


def hop(block, source, target):
    total = None
    for cross in range(HALVES):
        route = [
            (place(source, x, half), place(target, x, half ^ cross))
            for x in range(XS)
            for half in range(HALVES)
        ]
        got = lax.ppermute(block, ("s", "x", "zh"), route).astype(F32)
        total = got if total is None else total + got
    return jnp.broadcast_to(total.astype(BF16)[None], (XS,) + block.shape)


def pair_up(block, sections):
    route = [
        (place(s, x, half), place(s, x, 1 - half))
        for s in sections
        for x in range(XS)
        for half in range(HALVES)
    ]
    other = lax.ppermute(block, ("s", "x", "zh"), route)
    first = lax.axis_index("zh") == 0
    return jnp.concatenate([jnp.where(first, block, other), jnp.where(first, other, block)], -1)


def pick(items, station):
    chosen = items[0]
    for s in range(1, SECTIONS):
        chosen = jnp.where(station == s, items[s], chosen)
    return chosen


def shards(hidden_in, lengths, gains, w_query, w_keyval, w_out, grad_out):
    station = lax.axis_index("s")
    rows, length, shard = hidden_in.shape
    tokens = rows * length
    wq = w_query[0]
    width = wq.shape[0]
    wkv = w_keyval[0].reshape(width, -1)
    wo = w_out[0]
    block_width = width // XS
    qs, kvs = wq.shape[1], wkv.shape[1]
    flops = 2 * tokens * width * (2 * qs + kvs)
    tall = qs // HEAD_DIM * length

    start = jnp.where(
        station == 0, hidden_in.reshape(tokens, shard), grad_out.reshape(tokens, shard)
    )
    start = jnp.concatenate([start, jnp.broadcast_to(gains, (16, shard))], 0)
    start_block = pair_up(start, range(SECTIONS))
    start_full = gather_x(jnp.broadcast_to(start_block[None], (XS,) + start_block.shape))
    gain = start_full[:, tokens, :].reshape(1, width)
    first = start_full[:, :tokens]
    first_block = start_block[:tokens]

    shape = jax.ShapeDtypeStruct
    sent = shape((XS, tokens, block_width), BF16)
    saved = [
        shape((tokens, 1), F32),
        shape((tokens, qs), BF16),
        shape((tokens, kvs), BF16),
        shape((tokens, qs), BF16),
        shape((rows, tall, length), F32),
    ]
    held = [pltpu.VMEM((width, qs), BF16), pltpu.VMEM((width, kvs), BF16)]
    held_out = [pltpu.VMEM((qs, width), BF16)]

    kept = []
    parts, block = first, first_block
    for step in range(SECTIONS):
        if step:
            parts = gather_x(spread)
            block = spread[0]
        project = step + 1 < SECTIONS
        got = call(
            functools.partial(forward_kernel, rows, length, project),
            [sent] * project + saved,
            held + held_out * project,
            3 * XS,
            flops,
            (lengths, parts, gain, wq, wkv, wo),
        )
        kept.append((parts,) + tuple(got[project:]))
        if project:
            block = (0.5 * block.astype(F32) + scatter_x(got[0])).astype(BF16)
            spread = hop(block, step, step + 1)

    cut = lambda wide: wide.reshape(tokens, DP, width // DP).transpose(1, 0, 2)
    to_all = lambda narrow: jnp.broadcast_to(narrow[None], (DP,) + narrow.shape)
    half = width // DP
    over_dp = lambda v: lax.all_to_all(v, ("y", "core"), 0, 0)

    def early(items):
        picked, scale, mix = items
        gains_cut = gain.reshape(XS, 1, block_width).astype(F32)
        normed = (picked.astype(F32) * scale * gains_cut).astype(BF16)
        normed = normed.reshape(XS, tokens, 2, half).transpose(0, 2, 1, 3).reshape(DP, tokens, half)
        return over_dp(jnp.concatenate([normed, to_all(mix)], -1))

    def items_at(step):
        return kept[step][0], kept[step][1], kept[step][4]

    chosen = [
        jnp.where(station == 0, a, jnp.where(station == 1, b, c))
        for a, b, c in zip(items_at(0), items_at(1), items_at(2))
    ]
    factors = lax.cond(
        station < SECTIONS - 1,
        early,
        lambda items: jnp.zeros((DP, tokens, half + qs), BF16),
        chosen,
    )

    parts_grad, block = first, first_block
    last = None
    for step in reversed(range(SECTIONS)):
        if step + 1 < SECTIONS:
            parts_grad = gather_x(spread)
            block = spread[0]
        parts, scale, q, kv, mix, attn = kept[step]
        onward = step > 0
        got = call(
            functools.partial(backward_kernel, rows, length, onward),
            [sent] * onward
            + [shape((tokens, qs), BF16), shape((tokens, kvs), BF16), shape((1, width), F32)],
            held + held_out,
            3 * XS,
            flops,
            (parts_grad, parts, gain, scale, q, kv, attn, wq, wkv, wo),
        )
        found = (parts_grad,) + tuple(got[onward:])
        last = found if last is None else [jnp.where(station == step, a, b) for a, b in zip(found, last)]
        if onward:
            block = (0.5 * block.astype(F32) + scatter_x(got[0])).astype(BF16)
            spread = hop(block, step, step - 1)
        if step == SECTIONS - 1:
            factors = lax.cond(
                station == SECTIONS - 1, lambda items, kept_factors: early(items),
                lambda items, kept_factors: kept_factors, items_at(step), factors,
            )

    parts_grad, query_grad, pair_grad, gain_part = last
    send_g = parts_grad.reshape(XS, tokens, 2, half).transpose(0, 2, 1, 3).reshape(DP, tokens, half)
    full_grad = over_dp(send_g).reshape(DP * tokens, half)
    piece = width // (DP * XS * HALVES)
    pieces = gain_part.reshape(XS * HALVES, DP, piece).transpose(1, 0, 2).reshape(DP, 1, half)
    high = pieces.astype(BF16)
    low = (pieces - high.astype(F32)).astype(BF16)
    extra = jnp.concatenate([high, low, jnp.zeros((DP, 14, half), BF16)], 1)
    extra = jnp.concatenate([extra, jnp.zeros((DP, 16, qs + kvs - half), BF16)], -1)
    pair = jnp.concatenate([to_all(query_grad), to_all(pair_grad)], -1)
    got = over_dp(jnp.concatenate([pair, extra], 1))
    pieces = jnp.sum(got[:, tokens : tokens + 2, :half].astype(F32), (0, 1)).reshape(XS * HALVES, 1, piece)
    gain_grad = jnp.sum(lax.all_to_all(pieces, ("x", "zh"), 0, 0), 0)
    pair = got[:, :tokens].reshape(DP * tokens, -1)
    normed = factors[:, :, :half].reshape(DP * tokens, half)
    mix = factors[:, :, half:].reshape(DP * tokens, qs)
    grad_out_weight = dot(mix, full_grad, ((0,), (0,)))
    grad_query = dot(normed, pair[:, :qs], ((0,), (0,)))
    grad_pair = dot(normed, pair[:, qs:], ((0,), (0,)))
    return (
        grad_query[None],
        grad_pair.reshape(1, half, 1, -1),
        grad_out_weight[None],
        gain_grad[None][:, 0],
    )


def solution(mesh):
    grid = Mesh(mesh.devices.reshape(SECTIONS, XS, HALVES, 4, 2), ("s", "x", "zh", "y", "core"))
    section, tensor, dp = "s", ("x", "zh"), ("y", "core")
    in_specs = (
        P(dp, None, tensor),
        P(dp),
        P(section, tensor),
        P(section, None, tensor),
        P(section, None, tensor, None),
        P(section, tensor, None),
        P(dp, None, tensor),
    )
    out_specs = (
        P(section, dp, tensor),
        P(section, dp, tensor, None),
        P(section, tensor, dp),
        P(section, tensor + dp),
    )
    return jax.shard_map(shards, mesh=grid, in_specs=in_specs, out_specs=out_specs, check_vma=False)
```

```python
import functools

import jax
import jax.numpy as jnp
from jax import lax
from jax.experimental import pallas as pl
from jax.experimental.pallas import tpu as pltpu
from jax.sharding import Mesh, PartitionSpec as P

HEAD_DIM = 128
EPS = 1e-05
NEG = -1e30
F32 = jnp.float32
BF16 = jnp.bfloat16
SECTIONS, XS, HALVES, DP = 4, 4, 2, 8
VMEM = pl.BlockSpec(memory_space=pltpu.VMEM)
SMEM = pl.BlockSpec(memory_space=pltpu.SMEM)
HBM = pl.BlockSpec(memory_space=pltpu.HBM)


def dot(former, latter, dims=((1,), (0,))):
    return lax.dot_general(former, latter, (dims, ((), ())), preferred_element_type=F32)


def copies(pairs, sems):
    at = (lambda i: sems[i]) if isinstance(sems, list) else (lambda i: sems.at[i])
    return [pltpu.make_async_copy(a, b, at(i)) for i, (a, b) in enumerate(pairs)]


def heads_down(wide, row, length):
    part = wide[row * length : (row + 1) * length, :]
    return jnp.concatenate(
        [part[:, a : a + HEAD_DIM] for a in range(0, part.shape[1], HEAD_DIM)], axis=0
    )


def heads_across(tall, length):
    return jnp.concatenate(
        [tall[a : a + length] for a in range(0, tall.shape[0], length)], axis=1
    )


def forward_kernel(rows, length, project, lens, parts, gain, wq, wkv, wo, *rest):
    if project:
        send, rest = rest[0], rest[1:]
    pack, scale_out, q_out, kv_out, attn_out = rest[:5]
    wq_v, wkv_v, normed_v, mix_v, sems, out_sems = rest[5:11]
    wo_v = rest[11] if project else None
    block = parts.shape[2]
    width = XS * block
    piece = width // DP
    pairs = []
    for j in range(XS):
        span = pl.ds(j * block, block)
        pairs.append((wq.at[span], wq_v.at[span]))
        pairs.append((wkv.at[span], wkv_v.at[span]))
    if project:
        for j in range(XS):
            span = pl.ds(j * block, block)
            pairs.append((wo.at[:, span], wo_v.at[:, span]))
    moves = copies(pairs, sems)
    for move in moves:
        move.start()
    total = jnp.zeros((parts.shape[1], 1), F32)
    for j in range(XS):
        h = parts[j].astype(F32)
        total = total + jnp.sum(h * h, -1, keepdims=True)
    scale = lax.rsqrt(total / width + EPS)
    scale_out[...] = scale
    q = jnp.zeros(q_out.shape, F32)
    kv = jnp.zeros(kv_out.shape, F32)
    for j in range(XS):
        span = slice(j * block, (j + 1) * block)
        normed = (parts[j].astype(F32) * scale * gain[:, span].astype(F32)).astype(BF16)
        normed_v[:, span] = normed
        moves[2 * j].wait()
        q = q + dot(normed, wq_v[span, :])
        moves[2 * j + 1].wait()
        kv = kv + dot(normed, wkv_v[span, :])
    q = q.astype(BF16)
    kv = kv.astype(BF16)
    q_out[...] = q
    kv_out[...] = kv
    tall = q.shape[1] // HEAD_DIM * length
    at = lax.broadcasted_iota(jnp.int32, (tall, length), 0) % length
    key_at = lax.broadcasted_iota(jnp.int32, (tall, length), 1)
    mixes = []
    for row in range(rows):
        here = slice(row * length, (row + 1) * length)
        keys, values = kv[here, :HEAD_DIM], kv[here, HEAD_DIM:]
        scores = dot(heads_down(q, row, length), keys, ((1,), (1,))) * HEAD_DIM ** (-0.5)
        scores = jnp.where((key_at <= at) & (key_at < lens[row]), scores, NEG)
        raised = jnp.exp(scores - jnp.max(scores, -1, keepdims=True))
        attn = raised / jnp.sum(raised, -1, keepdims=True)
        attn_out[row] = attn
        mixes.append(heads_across(dot(attn.astype(BF16), values).astype(BF16), length))
    mix = jnp.concatenate(mixes, axis=0)
    mix_v[...] = mix
    outs = []
    for d in range(DP):
        outs.append((normed_v.at[:, pl.ds(d * piece, piece)], pack.at[d, :, pl.ds(0, piece)]))
        outs.append((mix_v, pack.at[d, :, pl.ds(piece, mix.shape[1])]))
    outs = copies(outs, out_sems)

    for move in outs:
        move.start()

    if project:
        for j in range(XS):
            moves[2 * XS + j].wait()
            send[j] = dot(mix, wo_v[:, j * block : (j + 1) * block]).astype(BF16)

    for move in outs:
        move.wait()


def backward_kernel(
    rows, length, onward, grads, parts, gain, scale_in, q_in, kv_in, attn_in,
    wq, wkv, wo, *rest
):
    if onward:
        send, rest = rest[0], rest[1:]
    pack, wq_v, wkv_v, wo_v, qg_v, pg_v, gain_v, gain_pair_v, sems, out_sems = rest
    tokens, block = parts.shape[1:]
    width = XS * block
    piece = width // DP
    qs, kvs = qg_v.shape[1], pg_v.shape[1]
    pairs = []
    for j in range(XS):
        span = pl.ds(j * block, block)
        pairs.append((wo.at[:, span], wo_v.at[:, span]))
    for j in range(XS):
        span = pl.ds(j * block, block)
        pairs.append((wq.at[span], wq_v.at[span]))
        pairs.append((wkv.at[span], wkv_v.at[span]))
    moves = copies(pairs, sems)
    for move in moves:
        move.start()
    real = pl.ds(0, tokens)
    outs = []
    for d in range(DP):
        outs.append(
            (grads.at[d // 2, :, pl.ds(d % 2 * piece, piece)], pack.at[d, real, pl.ds(0, piece)])
        )
    for d in range(DP):
        outs.append((qg_v, pack.at[d, real, pl.ds(piece, qs)]))
        outs.append((pg_v, pack.at[d, real, pl.ds(piece + qs, kvs)]))
    for d in range(DP):
        outs.append((gain_pair_v, pack.at[d, pl.ds(tokens, 16), pl.ds(0, piece)]))
    outs = copies(outs, out_sems)

    for move in outs[:DP]:
        move.start()

    mix_grad = jnp.zeros(q_in.shape, F32)
    for j in range(XS):
        moves[j].wait()
        mix_grad = mix_grad + dot(grads[j], wo_v[:, j * block : (j + 1) * block], ((1,), (1,)))
    mix_grad = mix_grad.astype(BF16)
    q = q_in[...]
    kv = kv_in[...]
    query_grads, pair_grads = [], []
    for row in range(rows):
        here = slice(row * length, (row + 1) * length)
        keys, values = kv[here, :HEAD_DIM], kv[here, HEAD_DIM:]
        attn = attn_in[row]
        mixed = heads_down(mix_grad, row, length)
        value_grad = dot(attn.astype(BF16), mixed, ((0,), (0,)))
        weight_grad = dot(mixed, values, ((1,), (1,)))
        score_grad = attn * (weight_grad - jnp.sum(weight_grad * attn, -1, keepdims=True))
        score_grad = (score_grad * HEAD_DIM ** (-0.5)).astype(BF16)
        query_grads.append(heads_across(dot(score_grad, keys).astype(BF16), length))
        key_grad = dot(score_grad, heads_down(q, row, length), ((0,), (0,)))
        pair_grads.append(jnp.concatenate([key_grad, value_grad], axis=1).astype(BF16))
    query_grad = jnp.concatenate(query_grads, axis=0)
    pair_grad = jnp.concatenate(pair_grads, axis=0)
    qg_v[...] = query_grad
    pg_v[...] = pair_grad

    for move in outs[DP : 3 * DP]:
        move.start()

    scale = scale_in[...]
    if onward:
        correction = jnp.sum(query_grad.astype(F32) * q.astype(F32), -1, keepdims=True)
        correction += jnp.sum(pair_grad.astype(F32) * kv.astype(F32), -1, keepdims=True)
        pull = scale * scale / width * correction
    for j in range(XS):
        span = slice(j * block, (j + 1) * block)
        moves[XS + 2 * j].wait()
        moves[XS + 2 * j + 1].wait()
        normed_grad = dot(query_grad, wq_v[span, :], ((1,), (1,))) + dot(
            pair_grad, wkv_v[span, :], ((1,), (1,))
        )
        h = parts[j].astype(F32)
        scaled = normed_grad * scale
        part = jnp.sum(scaled * h, 0, keepdims=True)
        gain_v[2 * j : 2 * j + 1, :] = part[:, :piece]
        gain_v[2 * j + 1 : 2 * j + 2, :] = part[:, piece:]
        if onward:
            send[j] = (scaled * gain[:, span].astype(F32) - h * pull).astype(BF16)
    terms = gain_v[...]
    high = terms.astype(BF16)
    low = (terms - high.astype(F32)).astype(BF16)
    gain_pair_v[...] = jnp.concatenate([high, low], axis=0)

    for move in outs[3 * DP :]:
        move.start()
    for move in outs:
        move.wait()


def weights_kernel(
    last, station, early, late, got, grad_query, grad_pair, grad_out, factors, wide_v, out_v, sem, sems
):
    tokens = early.shape[1]
    piece = grad_query.shape[0]
    qs = grad_query.shape[1]
    load = copies([(early, factors), (late, factors)], [sem.at[0], sem.at[0]])

    @pl.when(station[0] != last)
    def _():
        load[0].start()

    @pl.when(station[0] == last)
    def _():
        load[1].start()

    for d in range(DP):
        wide_v[d * tokens : (d + 1) * tokens, :] = got[d, :tokens, :]
    load[0].wait()
    flat = factors[...].reshape(DP * tokens, factors.shape[2])
    wide = wide_v[...]
    kvs = grad_pair.shape[1]
    out_v[:, :qs] = dot(flat[:, piece:], wide[:, :piece], ((0,), (0,)))
    outs = copies(
        [
            (out_v.at[:, pl.ds(0, piece)], grad_out),
            (out_v.at[:, pl.ds(piece, qs)], grad_query),
            (out_v.at[:, pl.ds(piece + qs, kvs)], grad_pair),
        ],
        sems,
    )
    outs[0].start()
    out_v[:, piece:] = dot(flat[:, :piece], wide[:, piece:], ((0,), (0,)))
    outs[1].start()
    outs[2].start()
    for move in outs:
        move.wait()


def combine_kernel(first, second, spread):
    total = (first[...].astype(F32) + second[...].astype(F32)).astype(BF16)
    for j in range(XS):
        spread[j] = total


def call(kernel, ins, outs, scratch, flops, args, aliases={}):
    return pl.pallas_call(
        kernel,
        out_shape=[out for out, _ in outs],
        in_specs=ins,
        out_specs=[spec for _, spec in outs],
        scratch_shapes=scratch,
        input_output_aliases=aliases,
        compiler_params=pltpu.CompilerParams(vmem_limit_bytes=40 * 2**20),
        cost_estimate=pl.CostEstimate(flops=flops, bytes_accessed=12 * 2**20, transcendentals=2**16),
    )(*args)


def place(section, x, half):
    return (section * XS + x) * HALVES + half


def gather_x(spread):
    return lax.all_to_all(spread, "x", 0, 0)


def scatter_x(parts):
    return jnp.sum(lax.all_to_all(parts, "x", 0, 0).astype(F32), 0)


def hop(block, source, target):
    got = []
    for cross in range(HALVES):
        route = [
            (place(source, x, half), place(target, x, half ^ cross))
            for x in range(XS)
            for half in range(HALVES)
        ]
        got.append(lax.ppermute(block, ("s", "x", "zh"), route))
    return got


def combine(first, second):
    spread = jax.ShapeDtypeStruct((XS,) + first.shape, BF16)
    return call(combine_kernel, [VMEM] * 2, [(spread, VMEM)], [], 2**20, (first, second))[0]


def nothing(*outs):
    return pl.pallas_call(
        lambda *refs: None, out_shape=[o for o, _ in outs], out_specs=[HBM for _ in outs]
    )()


def pair_up(block, sections):
    route = [
        (place(s, x, half), place(s, x, 1 - half))
        for s in sections
        for x in range(XS)
        for half in range(HALVES)
    ]
    other = lax.ppermute(block, ("s", "x", "zh"), route)
    first = lax.axis_index("zh") == 0
    return jnp.concatenate([jnp.where(first, block, other), jnp.where(first, other, block)], -1)


def shards(hidden_in, lengths, gains, w_query, w_keyval, w_out, grad_out):
    station = lax.axis_index("s")
    rows, length, shard = hidden_in.shape
    tokens = rows * length
    wq = w_query[0]
    width = wq.shape[0]
    wkv = w_keyval[0].reshape(width, -1)
    wo = w_out[0]
    block_width = width // XS
    qs, kvs = wq.shape[1], wkv.shape[1]
    flops = 2 * tokens * width * (2 * qs + kvs)
    tall = qs // HEAD_DIM * length

    start = jnp.where(
        station == 0, hidden_in.reshape(tokens, shard), grad_out.reshape(tokens, shard)
    )
    start = jnp.concatenate([start, jnp.broadcast_to(gains, (16, shard))], 0)
    start_block = pair_up(start, range(SECTIONS))
    start_full = gather_x(jnp.broadcast_to(start_block[None], (XS,) + start_block.shape))
    gain = start_full[:, tokens, :].reshape(1, width)
    first = start_full[:, :tokens]
    first_block = start_block[:tokens]

    shape = jax.ShapeDtypeStruct
    dma = lambda count: pltpu.SemaphoreType.DMA((count,))
    here = station.reshape(1)
    piece = width // DP
    sent = (shape((XS, tokens, block_width), BF16), VMEM)
    early_pack = (shape((DP, tokens, piece + qs), BF16), HBM)
    late_pack = (shape((DP, tokens + 16, piece + qs + kvs), BF16), HBM)
    saved = [
        (shape((tokens, 1), F32), VMEM),
        (shape((tokens, qs), BF16), VMEM),
        (shape((tokens, kvs), BF16), VMEM),
        (shape((rows, tall, length), F32), VMEM),
    ]
    held = [pltpu.VMEM((width, qs), BF16), pltpu.VMEM((width, kvs), BF16)]
    held_out = [pltpu.VMEM((qs, width), BF16)]
    over_dp = lambda v: lax.all_to_all(v, ("y", "core"), 0, 0)

    last_section = SECTIONS - 1
    block_out = (shape((tokens, block_width), BF16), HBM)
    factors_out = (shape((DP, tokens, piece + qs), BF16), HBM)
    parts_out = (shape((XS, tokens, block_width), BF16), HBM)

    def forward(parts, project):
        return call(
            functools.partial(forward_kernel, rows, length, project),
            [SMEM, VMEM, VMEM, HBM, HBM, HBM],
            [sent] * project + [early_pack] + saved,
            held
            + [pltpu.VMEM((tokens, width), BF16), pltpu.VMEM((tokens, qs), BF16)]
            + [dma(3 * XS), dma(2 * DP)]
            + held_out * project,
            flops,
            (lengths, parts, gain, wq, wkv, wo),
        )

    def backward(parts_grad, kept, onward):
        return call(
            functools.partial(backward_kernel, rows, length, onward),
            [VMEM] * 7 + [HBM] * 3,
            [sent] * onward + [late_pack],
            held
            + held_out
            + [pltpu.VMEM((tokens, qs), BF16), pltpu.VMEM((tokens, kvs), BF16)]
            + [pltpu.VMEM((DP, piece), F32), pltpu.VMEM((2 * DP, piece), BF16)]
            + [dma(3 * XS), dma(4 * DP)],
            flops,
            (parts_grad, kept[0], gain) + tuple(kept[1:]) + (wq, wkv, wo),
        )

    def pass_on(block, sums):
        return (0.5 * block.astype(F32) + scatter_x(sums)).astype(BF16)

    kept = []
    packed = None
    arrived = None
    for step in range(last_section):

        def work(packed, arrived):
            if arrived is None:
                parts, block = first, first_block
            else:
                spread = combine(*arrived)
                parts, block = gather_x(spread), spread[0]
            got = forward(parts, True)
            return pass_on(block, got[0]), got[1], [parts] + list(got[2:])

        def rest(packed, arrived):
            empty = nothing(block_out, early_pack, parts_out, *saved)
            return empty[0], empty[1] if packed is None else packed, list(empty[2:])

        block, packed, saved_here = lax.cond(station == step, work, rest, packed, arrived)
        kept.append(saved_here)
        arrived = hop(block, step, step + 1)

    def turn(packed, arrived):
        spread = combine(*arrived)
        parts = gather_x(spread)
        got = forward(parts, False)
        back = backward(first, [parts] + list(got[1:]), True)
        empty = nothing(factors_out)
        return pass_on(first_block, back[0]), back[1], got[0], empty[0]

    def exchange(packed, arrived):
        empty = nothing(block_out, late_pack, early_pack)
        return tuple(empty) + (over_dp(packed),)

    block, pack, late_factors, early = lax.cond(
        station == last_section, turn, exchange, packed, arrived
    )
    arrived = hop(block, last_section, last_section - 1)

    for step in reversed(range(last_section)):
        onward = step > 0
        if not onward:
            late = lax.cond(
                station == last_section, over_dp, lambda v: nothing(factors_out)[0], late_factors
            )
            late, *arrived = lax.optimization_barrier([late] + list(arrived))

        def work(pack, arrived, kept_here):
            spread = combine(*arrived)
            got = backward(gather_x(spread), kept_here, onward)
            return ([pass_on(spread[0], got[0])] if onward else []) + [got[onward]]

        def rest(pack, arrived, kept_here):
            return ([nothing(block_out)[0]] if onward else []) + [pack]

        got = lax.cond(station == step, work, rest, pack, arrived, kept[step])
        pack = got[-1]
        if onward:
            arrived = hop(got[0], step, step - 1)

    got = over_dp(pack)
    terms = got[:, tokens:, :piece].astype(F32).reshape(DP, 2, DP, piece)
    terms = jnp.sum(terms, (0, 1))
    small = piece // DP
    own = lax.axis_index(("y", "core")) * small
    terms = lax.dynamic_slice_in_dim(terms, own, small, 1).reshape(DP, 1, small)
    gain_grad = jnp.sum(lax.all_to_all(terms, ("x", "zh"), 0, 0), 0)
    grad_query, grad_pair, grad_out_weight = call(
        functools.partial(weights_kernel, last_section),
        [SMEM, HBM, HBM, VMEM],
        [
            (shape((piece, qs), F32), HBM),
            (shape((piece, kvs), F32), HBM),
            (shape((qs, piece), F32), HBM),
        ],
        [
            pltpu.VMEM((DP, tokens, piece + qs), BF16),
            pltpu.VMEM((DP * tokens, piece + qs + kvs), BF16),
            pltpu.VMEM((piece, piece + qs + kvs), F32),
            dma(1),
            dma(3),
        ],
        flops,
        (here, early, late, got),
    )
    return (
        grad_query[None],
        grad_pair.reshape(1, piece, 1, kvs),
        grad_out_weight[None],
        gain_grad[None][:, 0],
    )


def solution(mesh):
    grid = Mesh(mesh.devices.reshape(SECTIONS, XS, HALVES, 4, 2), ("s", "x", "zh", "y", "core"))
    section, tensor, dp = "s", ("x", "zh"), ("y", "core")
    in_specs = (
        P(dp, None, tensor),
        P(dp),
        P(section, tensor),
        P(section, None, tensor),
        P(section, None, tensor, None),
        P(section, tensor, None),
        P(dp, None, tensor),
    )
    out_specs = (
        P(section, dp, tensor),
        P(section, dp, tensor, None),
        P(section, tensor, dp),
        P(section, tensor + dp),
    )
    return jax.shard_map(shards, mesh=grid, in_specs=in_specs, out_specs=out_specs, check_vma=False)
```

```python
import functools

import jax
import jax.numpy as jnp
from jax import lax
from jax.experimental import pallas as pl
from jax.experimental.pallas import tpu as pltpu
from jax.sharding import Mesh, PartitionSpec as P

HEAD_DIM = 128
EPS = 1e-05
NEG = -1e30
F32 = jnp.float32
BF16 = jnp.bfloat16
SECTIONS, XS, HALVES, DP = 4, 4, 2, 8
VMEM = pl.BlockSpec(memory_space=pltpu.VMEM)
SMEM = pl.BlockSpec(memory_space=pltpu.SMEM)
HBM = pl.BlockSpec(memory_space=pltpu.HBM)


def dot(former, latter, dims=((1,), (0,))):
    return lax.dot_general(former, latter, (dims, ((), ())), preferred_element_type=F32)


def copies(pairs, sems):
    at = (lambda i: sems[i]) if isinstance(sems, list) else (lambda i: sems.at[i])
    return [pltpu.make_async_copy(a, b, at(i)) for i, (a, b) in enumerate(pairs)]


def heads_down(wide, row, length):
    part = wide[row * length : (row + 1) * length, :]
    return jnp.concatenate(
        [part[:, a : a + HEAD_DIM] for a in range(0, part.shape[1], HEAD_DIM)], axis=0
    )


def heads_across(tall, length):
    return jnp.concatenate(
        [tall[a : a + length] for a in range(0, tall.shape[0], length)], axis=1
    )


def forward_kernel(rows, length, project, lens, parts, gain, wq, wkv, wo, *rest):
    if project:
        send, rest = rest[0], rest[1:]
    pack, scale_out, q_out, kv_out, attn_out = rest[:5]
    wq_v, wkv_v, normed_v, mix_v, sems, out_sems = rest[5:11]
    wo_v = rest[11] if project else None
    block = parts.shape[2]
    width = XS * block
    piece = width // DP
    pairs = []
    for j in range(XS):
        span = pl.ds(j * block, block)
        pairs.append((wq.at[span], wq_v.at[span]))
        pairs.append((wkv.at[span], wkv_v.at[span]))
    if project:
        for j in range(XS):
            span = pl.ds(j * block, block)
            pairs.append((wo.at[:, span], wo_v.at[:, span]))
    moves = copies(pairs, sems)
    for move in moves:
        move.start()
    tokens = q_out.shape[0]
    outs = []
    for d in range(DP):
        outs.append((normed_v.at[:, pl.ds(d * piece, piece)], pack.at[d, :, pl.ds(0, piece)]))
    for d in range(DP):
        outs.append((mix_v, pack.at[d, :, pl.ds(piece, mix_v.shape[1])]))
    outs = copies(outs, out_sems)
    total = jnp.zeros((tokens, 1), F32)
    for j in range(XS):
        h = parts[j, :tokens, :].astype(F32)
        total = total + jnp.sum(h * h, -1, keepdims=True)
    scale = lax.rsqrt(total / width + EPS)
    scale_out[...] = scale
    q = jnp.zeros(q_out.shape, F32)
    kv = jnp.zeros(kv_out.shape, F32)
    for j in range(XS):
        span = slice(j * block, (j + 1) * block)
        normed = (parts[j, :tokens, :].astype(F32) * scale * gain[:, span].astype(F32)).astype(BF16)
        normed_v[:, span] = normed
        moves[2 * j].wait()
        q = q + dot(normed, wq_v[span, :])
        moves[2 * j + 1].wait()
        kv = kv + dot(normed, wkv_v[span, :])
    for move in outs[:DP]:
        move.start()
    q = q.astype(BF16)
    kv = kv.astype(BF16)
    q_out[...] = q
    kv_out[...] = kv
    tall = q.shape[1] // HEAD_DIM * length
    at = lax.broadcasted_iota(jnp.int32, (tall, length), 0) % length
    key_at = lax.broadcasted_iota(jnp.int32, (tall, length), 1)
    mixes = []
    for row in range(rows):
        here = slice(row * length, (row + 1) * length)
        keys, values = kv[here, :HEAD_DIM], kv[here, HEAD_DIM:]
        scores = dot(heads_down(q, row, length), keys, ((1,), (1,))) * HEAD_DIM ** (-0.5)
        scores = jnp.where((key_at <= at) & (key_at < lens[row]), scores, NEG)
        raised = jnp.exp(scores - jnp.max(scores, -1, keepdims=True))
        attn = raised / jnp.sum(raised, -1, keepdims=True)
        attn_out[row] = attn
        mixes.append(heads_across(dot(attn.astype(BF16), values).astype(BF16), length))
    mix = jnp.concatenate(mixes, axis=0)
    mix_v[...] = mix
    for move in outs[DP:]:
        move.start()
    if project:
        for j in range(XS):
            moves[2 * XS + j].wait()
            send[j] = dot(mix, wo_v[:, j * block : (j + 1) * block]).astype(BF16)

    for move in outs:
        move.wait()


def backward_kernel(
    rows, length, onward, grads, parts, gain, scale_in, q_in, kv_in, attn_in,
    wq, wkv, wo, *rest
):
    if onward:
        send, rest = rest[0], rest[1:]
    pack, wq_v, wkv_v, wo_v, qg_v, pg_v, gain_v, gain_pair_v, sems, out_sems = rest
    tokens, block = q_in.shape[0], parts.shape[2]
    width = XS * block
    piece = width // DP
    qs, kvs = qg_v.shape[1], pg_v.shape[1]
    pairs = []
    for j in range(XS):
        span = pl.ds(j * block, block)
        pairs.append((wo.at[:, span], wo_v.at[:, span]))
    for j in range(XS):
        span = pl.ds(j * block, block)
        pairs.append((wq.at[span], wq_v.at[span]))
        pairs.append((wkv.at[span], wkv_v.at[span]))
    moves = copies(pairs, sems)
    for move in moves:
        move.start()
    outs = []
    for d in range(XS):
        outs.append((qg_v, pack.at[d, pl.ds(0, tokens), pl.ds(0, qs)]))
        outs.append((pg_v, pack.at[d, pl.ds(0, tokens), pl.ds(qs, kvs)]))
    for d in range(XS):
        outs.append((gain_pair_v, pack.at[d, pl.ds(tokens, 2 * DP), pl.ds(0, piece)]))
    outs = copies(outs, out_sems)
    mix_grad = jnp.zeros(q_in.shape, F32)
    for j in range(XS):
        moves[j].wait()
        mix_grad = mix_grad + dot(grads[j, :tokens, :], wo_v[:, j * block : (j + 1) * block], ((1,), (1,)))
    mix_grad = mix_grad.astype(BF16)
    q = q_in[...]
    kv = kv_in[...]
    query_grads, pair_grads = [], []
    for row in range(rows):
        here = slice(row * length, (row + 1) * length)
        keys, values = kv[here, :HEAD_DIM], kv[here, HEAD_DIM:]
        attn = attn_in[row]
        mixed = heads_down(mix_grad, row, length)
        value_grad = dot(attn.astype(BF16), mixed, ((0,), (0,)))
        weight_grad = dot(mixed, values, ((1,), (1,)))
        score_grad = attn * (weight_grad - jnp.sum(weight_grad * attn, -1, keepdims=True))
        score_grad = (score_grad * HEAD_DIM ** (-0.5)).astype(BF16)
        query_grads.append(heads_across(dot(score_grad, keys).astype(BF16), length))
        key_grad = dot(score_grad, heads_down(q, row, length), ((0,), (0,)))
        pair_grads.append(jnp.concatenate([key_grad, value_grad], axis=1).astype(BF16))
    query_grad = jnp.concatenate(query_grads, axis=0)
    pair_grad = jnp.concatenate(pair_grads, axis=0)
    qg_v[...] = query_grad
    pg_v[...] = pair_grad

    for move in outs[: 2 * XS]:
        move.start()

    scale = scale_in[...]
    if onward:
        correction = jnp.sum(query_grad.astype(F32) * q.astype(F32), -1, keepdims=True)
        correction += jnp.sum(pair_grad.astype(F32) * kv.astype(F32), -1, keepdims=True)
        pull = scale * scale / width * correction
    for j in range(XS):
        span = slice(j * block, (j + 1) * block)
        moves[XS + 2 * j].wait()
        moves[XS + 2 * j + 1].wait()
        normed_grad = dot(query_grad, wq_v[span, :], ((1,), (1,))) + dot(
            pair_grad, wkv_v[span, :], ((1,), (1,))
        )
        h = parts[j, :tokens, :].astype(F32)
        scaled = normed_grad * scale
        part = jnp.sum(scaled * h, 0, keepdims=True)
        gain_v[2 * j : 2 * j + 1, :] = part[:, :piece]
        gain_v[2 * j + 1 : 2 * j + 2, :] = part[:, piece:]
        if onward:
            send[j] = (scaled * gain[:, span].astype(F32) - h * pull).astype(BF16)
    terms = gain_v[...]
    high = terms.astype(BF16)
    low = (terms - high.astype(F32)).astype(BF16)
    gain_pair_v[...] = jnp.concatenate([high, low], axis=0)

    for move in outs[2 * XS :]:
        move.start()
    for move in outs:
        move.wait()


def weights_kernel(last, own, here, early, late, g, grads, *rest):
    tokens = early.shape[1]
    count, piece = g.shape[0], early.shape[2] // 2
    qs = early.shape[2] - piece
    if own:
        total, factors, wide, sems = rest
    else:
        before, grad_query, grad_pair, grad_out, factors, wide, out_v, pair_v, sems, out_sems = rest
    core = here[1] if own else 1 - here[1]
    load = [
        copies([(source.at[2 * i + core], factors.at[i]) for i in range(count)], sems)
        for source in (early, late)
    ]

    @pl.when(here[0] != last)
    def _():
        for move in load[0]:
            move.start()

    @pl.when(here[0] == last)
    def _():
        for move in load[1]:
            move.start()

    for i in range(count):
        rows = slice(i * tokens, (i + 1) * tokens)
        part = g[i, :tokens, :]
        part = jnp.where(here[1] == 0, part[:, :piece], part[:, piece:])
        wide[rows, :piece] = part
        wide[rows, piece:] = grads[i, :tokens, :]
    for move in load[0]:
        move.wait()
    flat = factors[...].reshape(count * tokens, factors.shape[2])
    if own:
        total[:, :piece] = dot(flat[:, piece:], wide[:, :piece], ((0,), (0,)))
        total[:, piece:] = dot(flat[:, :piece], wide[:, piece:], ((0,), (0,)))
        return
    outs = copies(
        [
            (out_v.at[:, pl.ds(0, piece)], grad_out),
            (out_v.at[:, pl.ds(piece, qs)], grad_query),
            (pair_v, grad_pair),
        ],
        out_sems,
    )
    out_v[:, :piece] = before[:, :piece] + dot(flat[:, piece:], wide[:, :piece], ((0,), (0,)))
    outs[0].start()
    terms = before[:, piece:] + dot(flat[:, :piece], wide[:, piece:], ((0,), (0,)))
    out_v[:, piece:] = terms[:, :qs]
    outs[1].start()
    for i in range(terms.shape[1] // HEAD_DIM - qs // HEAD_DIM):
        at = qs + i * HEAD_DIM
        pair_v[pl.ds(i, piece, stride=2), :] = terms[:, at : at + HEAD_DIM]
    outs[2].start()
    for move in outs:
        move.wait()


def combine_kernel(first, second, spread):
    total = (first[...].astype(F32) + second[...].astype(F32)).astype(BF16)
    for j in range(XS):
        spread[j] = total


def call(kernel, ins, outs, scratch, flops, args, aliases={}):
    return pl.pallas_call(
        kernel,
        out_shape=[out for out, _ in outs],
        in_specs=ins,
        out_specs=[spec for _, spec in outs],
        scratch_shapes=scratch,
        input_output_aliases=aliases,
        compiler_params=pltpu.CompilerParams(vmem_limit_bytes=40 * 2**20),
        cost_estimate=pl.CostEstimate(flops=flops, bytes_accessed=12 * 2**20, transcendentals=2**16),
    )(*args)


def place(section, x, half):
    return (section * XS + x) * HALVES + half


def gather_x(spread):
    return lax.all_to_all(spread, "x", 0, 0)


def hop(block, source, target):
    got = []
    for cross in range(HALVES):
        route = [
            (place(source, x, half), place(target, x, half ^ cross))
            for x in range(XS)
            for half in range(HALVES)
        ]
        got.append(lax.ppermute(block, ("s", "x", "zh"), route))
    return got


def combine(first, second):
    spread = jax.ShapeDtypeStruct((XS,) + first.shape, BF16)
    return call(combine_kernel, [VMEM] * 2, [(spread, VMEM)], [], 2**20, (first, second))[0]


def nothing(*outs):
    return pl.pallas_call(
        lambda *refs: None, out_shape=[o for o, _ in outs], out_specs=[HBM for _ in outs]
    )()


def start_kernel(here, hidden, grads, gains, out):
    rows, length, _ = hidden.shape
    for row in range(rows):
        mine = jnp.where(here[0] == 0, hidden[row], grads[row])
        out[row * length : (row + 1) * length, :] = mine
    tall = (out.shape[0] - rows * length, out.shape[1])
    out[rows * length :, :] = jnp.broadcast_to(gains[...].astype(F32), tall).astype(BF16)


def pair_kernel(here, mine, other, spread):
    width = mine.shape[1]
    first = here[2] == 0
    left = jnp.where(first, mine[...], other[...])
    right = jnp.where(first, other[...], mine[...])
    for j in range(XS):
        spread[j, :, :width] = left
        spread[j, :, width:] = right


def sum_kernel(tokens, sums, block, out):
    total = 0.5 * block[0, :tokens, :].astype(F32)
    for j in range(XS):
        total = total + sums[j].astype(F32)
    out[...] = total.astype(BF16)


def pair_up(start, here):
    route = [
        (place(s, x, half), place(s, x, 1 - half))
        for s in range(SECTIONS)
        for x in range(XS)
        for half in range(HALVES)
    ]
    other = lax.ppermute(start, ("s", "x", "zh"), route)
    spread = jax.ShapeDtypeStruct((XS, start.shape[0], 2 * start.shape[1]), BF16)
    return call(pair_kernel, [SMEM, VMEM, VMEM], [(spread, VMEM)], [], 2**20, (here, start, other))[0]


def shards(hidden_in, lengths, gains, w_query, w_keyval, w_out, grad_out):
    station = lax.axis_index("s")
    rows, length, shard = hidden_in.shape
    tokens = rows * length
    wq = w_query[0]
    width = wq.shape[0]
    wkv = w_keyval[0].reshape(width, -1)
    wo = w_out[0]
    block_width = width // XS
    qs, kvs = wq.shape[1], wkv.shape[1]
    flops = 2 * tokens * width * (2 * qs + kvs)
    tall = qs // HEAD_DIM * length

    here = jnp.stack([station, lax.axis_index("core"), lax.axis_index("zh")])
    start = call(
        start_kernel,
        [SMEM] + [VMEM] * 3,
        [(jax.ShapeDtypeStruct((tokens + 16, shard), BF16), VMEM)],
        [],
        2**20,
        (here, hidden_in, grad_out, gains),
    )[0]
    start_spread = pair_up(start, here)
    start_full = gather_x(start_spread)
    first_block = start_spread
    gain = start_full[:, tokens, :].reshape(1, width)
    first = start_full

    shape = jax.ShapeDtypeStruct
    dma = lambda count: pltpu.SemaphoreType.DMA((count,))
    piece = width // DP
    sent = (shape((XS, tokens, block_width), BF16), VMEM)
    early_pack = (shape((DP, tokens, piece + qs), BF16), HBM)
    late_pack = (shape((XS, tokens + 2 * DP, qs + kvs), BF16), HBM)
    saved = [
        (shape((tokens, 1), F32), VMEM),
        (shape((tokens, qs), BF16), VMEM),
        (shape((tokens, kvs), BF16), VMEM),
        (shape((rows, tall, length), F32), VMEM),
    ]
    held = [pltpu.VMEM((width, qs), BF16), pltpu.VMEM((width, kvs), BF16)]
    held_out = [pltpu.VMEM((qs, width), BF16)]
    over_dp = lambda v: lax.all_to_all(v, ("y", "core"), 0, 0)

    last_section = SECTIONS - 1
    block_out = (shape((tokens, block_width), BF16), HBM)
    factors_out = (shape((DP, tokens, piece + qs), BF16), HBM)
    parts_out = (shape((XS, tokens, block_width), BF16), HBM)

    def forward(parts, project):
        return call(
            functools.partial(forward_kernel, rows, length, project),
            [SMEM, VMEM, VMEM, HBM, HBM, HBM],
            [sent] * project + [early_pack] + saved,
            held
            + [pltpu.VMEM((tokens, width), BF16), pltpu.VMEM((tokens, qs), BF16)]
            + [dma(3 * XS), dma(2 * DP)]
            + held_out * project,
            flops,
            (lengths, parts, gain, wq, wkv, wo),
        )

    def backward(parts_grad, kept, onward):
        return call(
            functools.partial(backward_kernel, rows, length, onward),
            [VMEM] * 7 + [HBM] * 3,
            [sent] * onward + [late_pack],
            held
            + held_out
            + [pltpu.VMEM((tokens, qs), BF16), pltpu.VMEM((tokens, kvs), BF16)]
            + [pltpu.VMEM((DP, piece), F32), pltpu.VMEM((2 * DP, piece), BF16)]
            + [dma(3 * XS), dma(3 * XS)],
            flops,
            (parts_grad, kept[0], gain) + tuple(kept[1:]) + (wq, wkv, wo),
        )

    def pass_on(block, sums):
        return call(
            functools.partial(sum_kernel, tokens),
            [VMEM] * 2,
            [(block_out[0], VMEM)],
            [],
            2**20,
            (gather_x(sums), block),
        )[0]

    kept = []
    packed = None
    arrived = None
    for step in range(last_section):

        def work(packed, arrived):
            if arrived is None:
                parts, block = first, first_block
            else:
                spread = combine(*arrived)
                parts, block = gather_x(spread), spread
            got = forward(parts, True)
            return pass_on(block, got[0]), got[1], [parts] * (step > 0) + list(got[2:])

        def rest(packed, arrived):
            empty = nothing(block_out, early_pack, *[parts_out] * (step > 0), *saved)
            return empty[0], empty[1] if packed is None else packed, list(empty[2:])

        block, packed, saved_here = lax.cond(station == step, work, rest, packed, arrived)
        kept.append(saved_here if step else [first] + saved_here)
        arrived = hop(block, step, step + 1)

    def turn(packed, arrived):
        spread = combine(*arrived)
        parts = gather_x(spread)
        got = forward(parts, False)
        back = backward(first, [parts] + list(got[1:]), True)
        empty = nothing(factors_out)
        return pass_on(first_block, back[0]), back[1], got[0], empty[0]

    def exchange(packed, arrived):
        empty = nothing(block_out, late_pack, early_pack)
        return tuple(empty) + (over_dp(packed),)

    block, pack, late_factors, early = lax.cond(
        station == last_section, turn, exchange, packed, arrived
    )
    arrived = hop(block, last_section, last_section - 1)

    over_y = lambda v: lax.all_to_all(v, "y", 0, 0)
    swap = lambda v: lax.ppermute(v, "core", [(0, 1), (1, 0)])
    g_kept = first[:, :tokens]
    for step in reversed(range(last_section)):
        onward = step > 0
        if not onward:
            late = lax.cond(
                station == last_section, over_dp, lambda v: nothing(factors_out)[0], late_factors
            )
            late, *arrived = lax.optimization_barrier([late] + list(arrived))

        def work(pack, g_kept, arrived, kept_here):
            spread = combine(*arrived)
            g = gather_x(spread)
            got = backward(g, kept_here, onward)
            if onward:
                return got[1], g, pass_on(spread, got[0])
            return got[0], over_y(g)

        def rest(pack, g_kept, arrived, kept_here):
            return (pack, g_kept, nothing(block_out)[0]) if onward else (pack, over_y(g_kept))

        got = lax.cond(station == step, work, rest, pack, g_kept, arrived, kept[step])
        pack, g_kept = got[:2]
        if onward:
            arrived = hop(got[2], step, step - 1)

    g_own = g_kept
    g_other = swap(g_own)
    own = over_y(pack)
    other = swap(own)
    terms = 0.0
    for item in (own, other):
        item = item[:, tokens:, :piece].astype(F32).reshape(XS, 2, DP, piece)
        terms = terms + jnp.sum(item, (0, 1))
    small = piece // DP
    terms = lax.dynamic_slice_in_dim(terms, lax.axis_index(("y", "core")) * small, small, 1)
    gain_grad = jnp.sum(lax.all_to_all(terms.reshape(DP, 1, small), ("x", "zh"), 0, 0), 0)
    everything = piece + qs + kvs
    scratch = [
        pltpu.VMEM((XS, tokens, piece + qs), BF16),
        pltpu.VMEM((XS * tokens, everything), BF16),
    ]
    total = call(
        functools.partial(weights_kernel, last_section, True),
        [SMEM, HBM, HBM, VMEM, VMEM],
        [(shape((piece, everything), F32), VMEM)],
        scratch + [dma(XS)],
        flops,
        (here, early, late, g_own, own),
    )[0]
    grad_query, grad_pair, grad_out_weight = call(
        functools.partial(weights_kernel, last_section, False),
        [SMEM, HBM, HBM, VMEM, VMEM, VMEM],
        [
            (shape((piece, qs), F32), HBM),
            (shape((piece * kvs // HEAD_DIM, HEAD_DIM), F32), HBM),
            (shape((qs, piece), F32), HBM),
        ],
        scratch
        + [
            pltpu.VMEM((piece, piece + qs), F32),
            pltpu.VMEM((piece * kvs // HEAD_DIM, HEAD_DIM), F32),
            dma(XS),
            dma(3),
        ],
        flops,
        (here, early, late, g_other, other, total),
    )
    return (
        grad_query[None],
        grad_pair.reshape(1, piece, 1, kvs),
        grad_out_weight[None],
        gain_grad[None][:, 0],
    )


def solution(mesh):
    grid = Mesh(mesh.devices.reshape(SECTIONS, XS, HALVES, 4, 2), ("s", "x", "zh", "y", "core"))
    section, tensor, dp = "s", ("x", "zh"), ("y", "core")
    in_specs = (
        P(dp, None, tensor),
        P(dp),
        P(section, tensor),
        P(section, None, tensor),
        P(section, None, tensor, None),
        P(section, tensor, None),
        P(dp, None, tensor),
    )
    out_specs = (
        P(section, dp, tensor),
        P(section, dp, tensor, None),
        P(section, tensor, dp),
        P(section, tensor + dp),
    )
    return jax.shard_map(shards, mesh=grid, in_specs=in_specs, out_specs=out_specs, check_vma=False)
```

```python
import functools

import jax
import jax.numpy as jnp
from jax import lax
from jax.experimental import pallas as pl
from jax.experimental.pallas import tpu as pltpu
from jax.sharding import Mesh, PartitionSpec as P

HEAD_DIM = 128
EPS = 1e-05
NEG = -1e30
F32 = jnp.float32
BF16 = jnp.bfloat16
SECTIONS, XS, HALVES, DP = 4, 4, 2, 8
VMEM = pl.BlockSpec(memory_space=pltpu.VMEM)
SMEM = pl.BlockSpec(memory_space=pltpu.SMEM)
HBM = pl.BlockSpec(memory_space=pltpu.HBM)


def dot(former, latter, dims=((1,), (0,))):
    return lax.dot_general(former, latter, (dims, ((), ())), preferred_element_type=F32)


def copies(pairs, sems):
    at = (lambda i: sems[i]) if isinstance(sems, list) else (lambda i: sems.at[i])
    return [pltpu.make_async_copy(a, b, at(i)) for i, (a, b) in enumerate(pairs)]


def heads_down(wide, row, length):
    part = wide[row * length : (row + 1) * length, :]
    return jnp.concatenate(
        [part[:, a : a + HEAD_DIM] for a in range(0, part.shape[1], HEAD_DIM)], axis=0
    )


def heads_across(tall, length):
    return jnp.concatenate(
        [tall[a : a + length] for a in range(0, tall.shape[0], length)], axis=1
    )


def forward_kernel(rows, length, project, lens, parts, gain, wq, wkv, wo, *rest):
    if project:
        send, rest = rest[0], rest[1:]
    pack, scale_out, q_out, kv_out, attn_out = rest[:5]
    normed_v, mix_v, out_sems = rest[5:]
    block = parts.shape[2]
    width = XS * block
    piece = width // DP
    tokens = q_out.shape[0]
    outs = []
    for d in range(DP):
        outs.append((normed_v.at[:, pl.ds(d * piece, piece)], pack.at[d, :, pl.ds(0, piece)]))
    for d in range(DP):
        outs.append((mix_v, pack.at[d, :, pl.ds(piece, mix_v.shape[1])]))
    outs = copies(outs, out_sems)
    total = jnp.zeros((tokens, 1), F32)
    for j in range(XS):
        h = parts[j, :tokens, :].astype(F32)
        total = total + jnp.sum(h * h, -1, keepdims=True)
    scale = lax.rsqrt(total / width + EPS)
    scale_out[...] = scale
    q = jnp.zeros(q_out.shape, F32)
    kv = jnp.zeros(kv_out.shape, F32)
    for j in range(XS):
        span = slice(j * block, (j + 1) * block)
        normed = (parts[j, :tokens, :].astype(F32) * scale * gain[:, span].astype(F32)).astype(BF16)
        normed_v[:, span] = normed
        q = q + dot(normed, wq[span, :])
        kv = kv + dot(normed, wkv[span, :])
    for move in outs[:DP]:
        move.start()
    q = q.astype(BF16)
    kv = kv.astype(BF16)
    q_out[...] = q
    kv_out[...] = kv
    tall = q.shape[1] // HEAD_DIM * length
    at = lax.broadcasted_iota(jnp.int32, (tall, length), 0) % length
    key_at = lax.broadcasted_iota(jnp.int32, (tall, length), 1)
    mixes = []
    for row in range(rows):
        here = slice(row * length, (row + 1) * length)
        keys, values = kv[here, :HEAD_DIM], kv[here, HEAD_DIM:]
        scores = dot(heads_down(q, row, length), keys, ((1,), (1,))) * HEAD_DIM ** (-0.5)
        scores = jnp.where((key_at <= at) & (key_at < lens[row]), scores, NEG)
        raised = jnp.exp(scores - jnp.max(scores, -1, keepdims=True))
        attn = raised / jnp.sum(raised, -1, keepdims=True)
        attn_out[row] = attn
        mixes.append(heads_across(dot(attn.astype(BF16), values).astype(BF16), length))
    mix = jnp.concatenate(mixes, axis=0)
    mix_v[...] = mix
    for move in outs[DP:]:
        move.start()
    if project:
        for j in range(XS):
            send[j] = dot(mix, wo[:, j * block : (j + 1) * block]).astype(BF16)

    for move in outs:
        move.wait()


def backward_kernel(
    rows, length, onward, grads, parts, gain, scale_in, q_in, kv_in, attn_in,
    wq, wkv, wo, *rest
):
    if onward:
        send, rest = rest[0], rest[1:]
    pack, qg_v, pg_v, gain_v, gain_pair_v, out_sems = rest
    tokens, block = q_in.shape[0], parts.shape[2]
    width = XS * block
    piece = width // DP
    qs, kvs = qg_v.shape[1], pg_v.shape[1]
    outs = []
    for d in range(XS):
        outs.append((qg_v, pack.at[d, pl.ds(0, tokens), pl.ds(0, qs)]))
        outs.append((pg_v, pack.at[d, pl.ds(0, tokens), pl.ds(qs, kvs)]))
    for d in range(XS):
        outs.append((gain_pair_v, pack.at[d, pl.ds(tokens, 2 * DP), pl.ds(0, piece)]))
    outs = copies(outs, out_sems)
    mix_grad = jnp.zeros(q_in.shape, F32)
    for j in range(XS):
        mix_grad = mix_grad + dot(grads[j, :tokens, :], wo[:, j * block : (j + 1) * block], ((1,), (1,)))
    mix_grad = mix_grad.astype(BF16)
    q = q_in[...]
    kv = kv_in[...]
    query_grads, pair_grads = [], []
    for row in range(rows):
        here = slice(row * length, (row + 1) * length)
        keys, values = kv[here, :HEAD_DIM], kv[here, HEAD_DIM:]
        attn = attn_in[row]
        mixed = heads_down(mix_grad, row, length)
        value_grad = dot(attn.astype(BF16), mixed, ((0,), (0,)))
        weight_grad = dot(mixed, values, ((1,), (1,)))
        score_grad = attn * (weight_grad - jnp.sum(weight_grad * attn, -1, keepdims=True))
        score_grad = (score_grad * HEAD_DIM ** (-0.5)).astype(BF16)
        query_grads.append(heads_across(dot(score_grad, keys).astype(BF16), length))
        key_grad = dot(score_grad, heads_down(q, row, length), ((0,), (0,)))
        pair_grads.append(jnp.concatenate([key_grad, value_grad], axis=1).astype(BF16))
    query_grad = jnp.concatenate(query_grads, axis=0)
    pair_grad = jnp.concatenate(pair_grads, axis=0)
    qg_v[...] = query_grad
    pg_v[...] = pair_grad

    for move in outs[: 2 * XS]:
        move.start()

    scale = scale_in[...]
    if onward:
        correction = jnp.sum(query_grad.astype(F32) * q.astype(F32), -1, keepdims=True)
        correction += jnp.sum(pair_grad.astype(F32) * kv.astype(F32), -1, keepdims=True)
        pull = scale * scale / width * correction
    for j in range(XS):
        span = slice(j * block, (j + 1) * block)
        normed_grad = dot(query_grad, wq[span, :], ((1,), (1,))) + dot(
            pair_grad, wkv[span, :], ((1,), (1,))
        )
        h = parts[j, :tokens, :].astype(F32)
        scaled = normed_grad * scale
        part = jnp.sum(scaled * h, 0, keepdims=True)
        gain_v[2 * j : 2 * j + 1, :] = part[:, :piece]
        gain_v[2 * j + 1 : 2 * j + 2, :] = part[:, piece:]
        if onward:
            send[j] = (scaled * gain[:, span].astype(F32) - h * pull).astype(BF16)
    terms = gain_v[...]
    high = terms.astype(BF16)
    low = (terms - high.astype(F32)).astype(BF16)
    gain_pair_v[...] = jnp.concatenate([high, low], axis=0)

    for move in outs[2 * XS :]:
        move.start()
    for move in outs:
        move.wait()


def weights_kernel(last, own, here, early, late, g, grads, *rest):
    tokens = early.shape[1]
    count, piece = g.shape[0], early.shape[2] // 2
    qs = early.shape[2] - piece
    if own:
        total, factors, wide, sems = rest
    else:
        before, grad_query, grad_pair, grad_out, factors, wide, out_v, pair_v, sems, out_sems = rest
    core = here[1] if own else 1 - here[1]
    load = [
        copies([(source.at[2 * i + core], factors.at[i]) for i in range(count)], sems)
        for source in (early, late)
    ]

    @pl.when(here[0] != last)
    def _():
        for move in load[0]:
            move.start()

    @pl.when(here[0] == last)
    def _():
        for move in load[1]:
            move.start()

    for i in range(count):
        rows = slice(i * tokens, (i + 1) * tokens)
        part = g[i, :tokens, :]
        part = jnp.where(here[1] == 0, part[:, :piece], part[:, piece:])
        wide[rows, :piece] = part
        wide[rows, piece:] = grads[i, :tokens, :]
    for move in load[0]:
        move.wait()
    flat = factors[...].reshape(count * tokens, factors.shape[2])
    if own:
        total[:, :piece] = dot(flat[:, piece:], wide[:, :piece], ((0,), (0,)))
        total[:, piece:] = dot(flat[:, :piece], wide[:, piece:], ((0,), (0,)))
        return
    outs = copies(
        [
            (out_v.at[:, pl.ds(0, piece)], grad_out),
            (out_v.at[:, pl.ds(piece, qs)], grad_query),
            (pair_v, grad_pair),
        ],
        out_sems,
    )
    out_v[:, :piece] = before[:, :piece] + dot(flat[:, piece:], wide[:, :piece], ((0,), (0,)))
    outs[0].start()
    terms = before[:, piece:] + dot(flat[:, :piece], wide[:, piece:], ((0,), (0,)))
    out_v[:, piece:] = terms[:, :qs]
    outs[1].start()
    for i in range(terms.shape[1] // HEAD_DIM - qs // HEAD_DIM):
        at = qs + i * HEAD_DIM
        pair_v[pl.ds(i, piece, stride=2), :] = terms[:, at : at + HEAD_DIM]
    outs[2].start()
    for move in outs:
        move.wait()


def combine_kernel(first, second, wq, wo, spread):
    total = (first[...].astype(F32) + second[...].astype(F32)).astype(BF16)
    for j in range(XS):
        spread[j] = total


def call(kernel, ins, outs, scratch, flops, args, traffic=12 * 2**20):
    return pl.pallas_call(
        kernel,
        out_shape=[out for out, _ in outs],
        in_specs=ins,
        out_specs=[spec for _, spec in outs],
        scratch_shapes=scratch,
        compiler_params=pltpu.CompilerParams(vmem_limit_bytes=24 * 2**20),
        cost_estimate=pl.CostEstimate(flops=flops, bytes_accessed=traffic, transcendentals=2**16),
    )(*args)


def place(section, x, half):
    return (section * XS + x) * HALVES + half


def gather_x(spread):
    return lax.all_to_all(spread, "x", 0, 0)


def hop(block, source, target):
    got = []
    for cross in range(HALVES):
        route = [
            (place(source, x, half), place(target, x, half ^ cross))
            for x in range(XS)
            for half in range(HALVES)
        ]
        got.append(lax.ppermute(block, ("s", "x", "zh"), route))
    return got


def combine(first, second, wq, wo):
    spread = jax.ShapeDtypeStruct((XS,) + first.shape, BF16)
    return call(
        combine_kernel,
        [VMEM] * 2 + [pl.BlockSpec(memory_space=pl.ANY)] * 2,
        [(spread, VMEM)],
        [],
        2**20,
        (first, second, wq, wo),
        2**27,
    )[0]


def nothing(*outs):
    got = pl.pallas_call(
        lambda *refs: None, out_shape=[o for o, _ in outs], out_specs=[HBM for _ in outs]
    )()
    return list(got)


def pair_kernel(here, mine, other, spread):
    width = mine.shape[1]
    first = here[2] == 0
    left = jnp.where(first, mine[...], other[...])
    right = jnp.where(first, other[...], mine[...])
    for j in range(XS):
        spread[j, :, :width] = left
        spread[j, :, width:] = right


def sum_kernel(tokens, sums, block, out):
    total = 0.5 * block[0, :tokens, :].astype(F32)
    for j in range(XS):
        total = total + sums[j].astype(F32)
    out[...] = total.astype(BF16)


def pair_up(start, here):
    route = [
        (place(s, x, half), place(s, x, 1 - half))
        for s in range(SECTIONS)
        for x in range(XS)
        for half in range(HALVES)
    ]
    other = lax.ppermute(start, ("s", "x", "zh"), route)
    spread = jax.ShapeDtypeStruct((XS, start.shape[0], 2 * start.shape[1]), BF16)
    return call(pair_kernel, [SMEM, VMEM, VMEM], [(spread, VMEM)], [], 2**20, (here, start, other))[0]


def shards(hidden_in, lengths, gains, w_query, w_keyval, w_out, grad_out):
    station = lax.axis_index("s")
    rows, length, shard = hidden_in.shape
    tokens = rows * length
    wq = w_query[0]
    width = wq.shape[0]
    wkv = w_keyval[0].reshape(width, -1)
    wo = w_out[0]
    block_width = width // XS
    qs, kvs = wq.shape[1], wkv.shape[1]
    flops = 2 * tokens * width * (2 * qs + kvs)
    tall = qs // HEAD_DIM * length

    here = jnp.stack([station, lax.axis_index("core"), lax.axis_index("zh")])
    start = jnp.where(
        station == 0, hidden_in.reshape(tokens, shard), grad_out.reshape(tokens, shard)
    )
    start = jnp.concatenate([start, jnp.broadcast_to(gains, (16, shard))], 0)
    start_spread = pair_up(start, here)
    start_full, station = lax.optimization_barrier((gather_x(start_spread), station))
    first_block = start_spread
    gain = start_full[:, tokens, :].reshape(1, width)
    first = start_full

    shape = jax.ShapeDtypeStruct
    dma = lambda count: pltpu.SemaphoreType.DMA((count,))
    piece = width // DP
    sent = (shape((XS, tokens, block_width), BF16), VMEM)
    early_pack = (shape((DP, tokens, piece + qs), BF16), HBM)
    late_pack = (shape((XS, tokens + 2 * DP, qs + kvs), BF16), HBM)
    saved = [
        (shape((tokens, 1), F32), VMEM),
        (shape((tokens, qs), BF16), VMEM),
        (shape((tokens, kvs), BF16), VMEM),
        (shape((rows, tall, length), F32), VMEM),
    ]
    over_dp = lambda v: lax.all_to_all(v, ("y", "core"), 0, 0)

    last_section = SECTIONS - 1
    block_out = (shape((tokens, block_width), BF16), HBM)
    factors_out = (shape((DP, tokens, piece + qs), BF16), HBM)
    parts_out = (shape((XS, tokens, block_width), BF16), HBM)

    def forward(parts, project):
        return call(
            functools.partial(forward_kernel, rows, length, project),
            [SMEM] + [VMEM] * 5,
            [sent] * project + [early_pack] + saved,
            [pltpu.VMEM((tokens, width), BF16), pltpu.VMEM((tokens, qs), BF16), dma(2 * DP)],
            flops,
            (lengths, parts, gain, wq, wkv, wo),
        )

    def backward(parts_grad, kept, onward):
        return call(
            functools.partial(backward_kernel, rows, length, onward),
            [VMEM] * 10,
            [sent] * onward + [late_pack],
            [pltpu.VMEM((tokens, qs), BF16), pltpu.VMEM((tokens, kvs), BF16)]
            + [pltpu.VMEM((DP, piece), F32), pltpu.VMEM((2 * DP, piece), BF16), dma(3 * XS)],
            flops,
            (parts_grad, kept[0], gain) + tuple(kept[1:]) + (wq, wkv, wo),
        )

    def pass_on(block, sums):
        return call(
            functools.partial(sum_kernel, tokens),
            [VMEM] * 2,
            [(block_out[0], VMEM)],
            [],
            2**20,
            (gather_x(sums), block),
        )[0]

    kept = []
    packed = None
    arrived = None
    for step in range(last_section):

        def work(packed, arrived):
            if arrived is None:
                parts, block = first, first_block
            else:
                spread = combine(*arrived, wq, wo)
                parts, block = gather_x(spread), spread
            got = forward(parts, True)
            return pass_on(block, got[0]), got[1], [parts] * (step > 0) + list(got[2:])

        def rest(packed, arrived):
            empty = nothing(block_out, early_pack, *[parts_out] * (step > 0), *saved)
            return empty[0], empty[1] if packed is None else packed, list(empty[2:])

        block, packed, saved_here = lax.cond(station == step, work, rest, packed, arrived)
        kept.append(saved_here if step else [first] + saved_here)
        arrived = hop(block, step, step + 1)

    def turn(packed, arrived):
        empty, *arrived = lax.optimization_barrier(nothing(factors_out) + list(arrived))
        spread = combine(*arrived, wq, wo)
        parts = gather_x(spread)
        got = forward(parts, False)
        back = backward(first, [parts] + list(got[1:]), True)
        return pass_on(first_block, back[0]), back[1], got[0], empty

    def exchange(packed, arrived):
        empty = nothing(block_out, late_pack, early_pack)
        return tuple(empty) + (over_dp(packed),)

    block, pack, late_factors, early = lax.cond(
        station == last_section, turn, exchange, packed, arrived
    )
    arrived = hop(block, last_section, last_section - 1)

    over_y = lambda v: lax.all_to_all(v, "y", 0, 0)
    swap = lambda v: lax.ppermute(v, "core", [(0, 1), (1, 0)])
    g_kept = first[:, :tokens]
    for step in reversed(range(last_section)):
        onward = step > 0
        if not onward:
            late = lax.cond(
                station == last_section, over_dp, lambda v: nothing(factors_out)[0], late_factors
            )
            late, *arrived = lax.optimization_barrier([late] + list(arrived))

        def work(pack, g_kept, arrived, kept_here):
            spread = combine(*arrived, wq, wo)
            g = gather_x(spread)
            got = backward(g, kept_here, onward)
            if onward:
                return got[1], g, pass_on(spread, got[0])
            return got[0], over_y(g)

        def rest(pack, g_kept, arrived, kept_here):
            return (pack, g_kept, nothing(block_out)[0]) if onward else (pack, over_y(g_kept))

        got = lax.cond(station == step, work, rest, pack, g_kept, arrived, kept[step])
        pack, g_kept = got[:2]
        if onward:
            arrived = hop(got[2], step, step - 1)

    g_own = g_kept
    g_other = swap(g_own)
    own = over_y(pack)
    other = swap(own)
    terms = 0.0
    for item in (own, other):
        item = item[:, tokens:, :piece].astype(F32).reshape(XS, 2, DP, piece)
        terms = terms + jnp.sum(item, (0, 1))
    small = piece // DP
    terms = lax.dynamic_slice_in_dim(terms, lax.axis_index(("y", "core")) * small, small, 1)
    gain_grad = jnp.sum(lax.all_to_all(terms.reshape(DP, 1, small), ("x", "zh"), 0, 0), 0)
    everything = piece + qs + kvs
    scratch = [
        pltpu.VMEM((XS, tokens, piece + qs), BF16),
        pltpu.VMEM((XS * tokens, everything), BF16),
    ]
    total = call(
        functools.partial(weights_kernel, last_section, True),
        [SMEM, HBM, HBM, VMEM, VMEM],
        [(shape((piece, everything), F32), VMEM)],
        scratch + [dma(XS)],
        flops,
        (here, early, late, g_own, own),
    )[0]
    grad_query, grad_pair, grad_out_weight = call(
        functools.partial(weights_kernel, last_section, False),
        [SMEM, HBM, HBM, VMEM, VMEM, VMEM],
        [
            (shape((piece, qs), F32), HBM),
            (shape((piece * kvs // HEAD_DIM, HEAD_DIM), F32), HBM),
            (shape((qs, piece), F32), HBM),
        ],
        scratch
        + [
            pltpu.VMEM((piece, piece + qs), F32),
            pltpu.VMEM((piece * kvs // HEAD_DIM, HEAD_DIM), F32),
            dma(XS),
            dma(3),
        ],
        flops,
        (here, early, late, g_other, other, total),
    )
    return (
        grad_query[None],
        grad_pair.reshape(1, piece, 1, kvs),
        grad_out_weight[None],
        gain_grad[None][:, 0],
    )


def solution(mesh):
    grid = Mesh(mesh.devices.reshape(SECTIONS, XS, HALVES, 4, 2), ("s", "x", "zh", "y", "core"))
    section, tensor, dp = "s", ("x", "zh"), ("y", "core")
    in_specs = (
        P(dp, None, tensor),
        P(dp),
        P(section, tensor),
        P(section, None, tensor),
        P(section, None, tensor, None),
        P(section, tensor, None),
        P(dp, None, tensor),
    )
    out_specs = (
        P(section, dp, tensor),
        P(section, dp, tensor, None),
        P(section, tensor, dp),
        P(section, tensor + dp),
    )
    return jax.shard_map(shards, mesh=grid, in_specs=in_specs, out_specs=out_specs, check_vma=False)
```

```python
import functools

import jax
import jax.numpy as jnp
from jax import lax
from jax.experimental import pallas as pl
from jax.experimental.pallas import tpu as pltpu
from jax.sharding import Mesh, PartitionSpec as P

HEAD_DIM = 128
EPS = 1e-05
NEG = -1e30
F32 = jnp.float32
BF16 = jnp.bfloat16
SECTIONS, XS, HALVES, DP = 4, 4, 2, 8
VMEM = pl.BlockSpec(memory_space=pltpu.VMEM)
SMEM = pl.BlockSpec(memory_space=pltpu.SMEM)
HBM = pl.BlockSpec(memory_space=pltpu.HBM)


def dot(former, latter, dims=((1,), (0,))):
    return lax.dot_general(former, latter, (dims, ((), ())), preferred_element_type=F32)


def copies(pairs, sems):
    at = (lambda i: sems[i]) if isinstance(sems, list) else (lambda i: sems.at[i])
    return [pltpu.make_async_copy(a, b, at(i)) for i, (a, b) in enumerate(pairs)]


def heads_down(wide, row, length):
    part = wide[row * length : (row + 1) * length, :]
    return jnp.concatenate(
        [part[:, a : a + HEAD_DIM] for a in range(0, part.shape[1], HEAD_DIM)], axis=0
    )


def heads_across(tall, length):
    return jnp.concatenate(
        [tall[a : a + length] for a in range(0, tall.shape[0], length)], axis=1
    )


def forward_kernel(rows, length, project, arrive, lens, parts, gain, wq, wkv, wo, *rest):
    if project:
        send, rest = rest[0], rest[1:]
    pack, scale_out, q_out, kv_out, attn_out = rest[:5]
    normed_v, mix_v, out_sems = rest[5:]
    block = parts.shape[2]
    width = XS * block
    piece = width // DP
    tokens = q_out.shape[0]
    outs = []
    for d in range(DP):
        outs.append((normed_v.at[:, pl.ds(d * piece, piece)], pack.at[d, :, pl.ds(0, piece)]))
    for d in range(DP):
        outs.append((mix_v, pack.at[d, :, pl.ds(piece, mix_v.shape[1])]))
    outs = copies(outs, out_sems)
    total = jnp.zeros((tokens, 1), F32)
    for j in range(XS):
        h = parts[j, :tokens, :].astype(F32)
        total = total + jnp.sum(h * h, -1, keepdims=True)
    scale = lax.rsqrt(total / width + EPS)
    scale_out[...] = scale
    q = jnp.zeros(q_out.shape, F32)
    kv = jnp.zeros(kv_out.shape, F32)
    for j in range(XS):
        span = slice(j * block, (j + 1) * block)
        normed = (parts[j, :tokens, :].astype(F32) * scale * gain[:, span].astype(F32)).astype(BF16)
        normed_v[:, span] = normed
        arrive(j)
        q = q + dot(normed, wq[span, :])
        kv = kv + dot(normed, wkv[span, :])
    for move in outs[:DP]:
        move.start()
    q = q.astype(BF16)
    kv = kv.astype(BF16)
    q_out[...] = q
    kv_out[...] = kv
    tall = q.shape[1] // HEAD_DIM * length
    at = lax.broadcasted_iota(jnp.int32, (tall, length), 0) % length
    key_at = lax.broadcasted_iota(jnp.int32, (tall, length), 1)
    mixes = []
    for row in range(rows):
        here = slice(row * length, (row + 1) * length)
        keys, values = kv[here, :HEAD_DIM], kv[here, HEAD_DIM:]
        scores = dot(heads_down(q, row, length), keys, ((1,), (1,))) * HEAD_DIM ** (-0.5)
        scores = jnp.where((key_at <= at) & (key_at < lens[row]), scores, NEG)
        raised = jnp.exp(scores - jnp.max(scores, -1, keepdims=True))
        attn = raised / jnp.sum(raised, -1, keepdims=True)
        attn_out[row] = attn
        mixes.append(heads_across(dot(attn.astype(BF16), values).astype(BF16), length))
    mix = jnp.concatenate(mixes, axis=0)
    mix_v[...] = mix
    for move in outs[DP:]:
        move.start()
    if project:
        for j in range(XS):
            arrive(XS + j)
            send[j] = dot(mix, wo[:, j * block : (j + 1) * block]).astype(BF16)

    for move in outs:
        move.wait()


def backward_kernel(
    rows, length, onward, arrive, grads, parts, gain, scale_in, q_in, kv_in, attn_in,
    wq, wkv, wo, *rest
):
    if onward:
        send, rest = rest[0], rest[1:]
    pack, qg_v, pg_v, gain_v, gain_pair_v, out_sems = rest
    tokens, block = q_in.shape[0], parts.shape[2]
    width = XS * block
    piece = width // DP
    qs, kvs = qg_v.shape[1], pg_v.shape[1]
    outs = []
    for d in range(XS):
        outs.append((qg_v, pack.at[d, pl.ds(0, tokens), pl.ds(0, qs)]))
        outs.append((pg_v, pack.at[d, pl.ds(0, tokens), pl.ds(qs, kvs)]))
    for d in range(XS):
        outs.append((gain_pair_v, pack.at[d, pl.ds(tokens, 2 * DP), pl.ds(0, piece)]))
    outs = copies(outs, out_sems)
    mix_grad = jnp.zeros(q_in.shape, F32)
    for j in range(XS):
        arrive(XS + j)
        mix_grad = mix_grad + dot(grads[j, :tokens, :], wo[:, j * block : (j + 1) * block], ((1,), (1,)))
    mix_grad = mix_grad.astype(BF16)
    q = q_in[...]
    kv = kv_in[...]
    query_grads, pair_grads = [], []
    for row in range(rows):
        here = slice(row * length, (row + 1) * length)
        keys, values = kv[here, :HEAD_DIM], kv[here, HEAD_DIM:]
        attn = attn_in[row]
        mixed = heads_down(mix_grad, row, length)
        value_grad = dot(attn.astype(BF16), mixed, ((0,), (0,)))
        weight_grad = dot(mixed, values, ((1,), (1,)))
        score_grad = attn * (weight_grad - jnp.sum(weight_grad * attn, -1, keepdims=True))
        score_grad = (score_grad * HEAD_DIM ** (-0.5)).astype(BF16)
        query_grads.append(heads_across(dot(score_grad, keys).astype(BF16), length))
        key_grad = dot(score_grad, heads_down(q, row, length), ((0,), (0,)))
        pair_grads.append(jnp.concatenate([key_grad, value_grad], axis=1).astype(BF16))
    query_grad = jnp.concatenate(query_grads, axis=0)
    pair_grad = jnp.concatenate(pair_grads, axis=0)
    qg_v[...] = query_grad
    pg_v[...] = pair_grad

    for move in outs[: 2 * XS]:
        move.start()

    scale = scale_in[...]
    if onward:
        correction = jnp.sum(query_grad.astype(F32) * q.astype(F32), -1, keepdims=True)
        correction += jnp.sum(pair_grad.astype(F32) * kv.astype(F32), -1, keepdims=True)
        pull = scale * scale / width * correction
    for j in range(XS):
        span = slice(j * block, (j + 1) * block)
        arrive(j)
        normed_grad = dot(query_grad, wq[span, :], ((1,), (1,))) + dot(
            pair_grad, wkv[span, :], ((1,), (1,))
        )
        h = parts[j, :tokens, :].astype(F32)
        scaled = normed_grad * scale
        part = jnp.sum(scaled * h, 0, keepdims=True)
        gain_v[2 * j : 2 * j + 1, :] = part[:, :piece]
        gain_v[2 * j + 1 : 2 * j + 2, :] = part[:, piece:]
        if onward:
            send[j] = (scaled * gain[:, span].astype(F32) - h * pull).astype(BF16)
    terms = gain_v[...]
    high = terms.astype(BF16)
    low = (terms - high.astype(F32)).astype(BF16)
    gain_pair_v[...] = jnp.concatenate([high, low], axis=0)

    for move in outs[2 * XS :]:
        move.start()
    for move in outs:
        move.wait()


def streamed(kernel, rows, length, flag, out_first, *refs):
    *refs, wq_v, wo_v, sems = refs
    at = 3 if flag and not out_first else 7
    wq, wo = refs[at], refs[at + 2]
    block = wq.shape[0] // XS
    spans = [pl.ds(j * block, block) for j in range(XS)]
    pairs = [(wq.at[span], wq_v.at[span]) for span in spans]
    pairs += [(wo.at[:, span], wo_v.at[:, span]) for span in spans]
    moves = copies(pairs, sems)
    for move in moves[XS:] + moves[:XS] if out_first else moves:
        move.start()
    refs[at], refs[at + 2] = wq_v, wo_v
    kernel(rows, length, flag, lambda i: moves[i].wait(), *refs)


def weights_kernel(last, own, here, early, late, g, grads, *rest):
    tokens = early.shape[1]
    count, piece = g.shape[0], early.shape[2] // 2
    qs = early.shape[2] - piece
    if own:
        total, factors, wide, sems = rest
    else:
        before, grad_query, grad_pair, grad_out, factors, wide, out_v, pair_v, sems, out_sems = rest
    core = here[1] if own else 1 - here[1]
    load = [
        copies([(source.at[2 * i + core], factors.at[i]) for i in range(count)], sems)
        for source in (early, late)
    ]

    @pl.when(here[0] != last)
    def _():
        for move in load[0]:
            move.start()

    @pl.when(here[0] == last)
    def _():
        for move in load[1]:
            move.start()

    for i in range(count):
        rows = slice(i * tokens, (i + 1) * tokens)
        part = g[i, :tokens, :]
        part = jnp.where(here[1] == 0, part[:, :piece], part[:, piece:])
        wide[rows, :piece] = part
        wide[rows, piece:] = grads[i, :tokens, :]
    for move in load[0]:
        move.wait()
    flat = factors[...].reshape(count * tokens, factors.shape[2])
    if own:
        total[:, :piece] = dot(flat[:, piece:], wide[:, :piece], ((0,), (0,)))
        total[:, piece:] = dot(flat[:, :piece], wide[:, piece:], ((0,), (0,)))
        return
    outs = copies(
        [
            (out_v.at[:, pl.ds(0, piece)], grad_out),
            (out_v.at[:, pl.ds(piece, qs)], grad_query),
            (pair_v, grad_pair),
        ],
        out_sems,
    )
    out_v[:, :piece] = before[:, :piece] + dot(flat[:, piece:], wide[:, :piece], ((0,), (0,)))
    outs[0].start()
    terms = before[:, piece:] + dot(flat[:, :piece], wide[:, piece:], ((0,), (0,)))
    out_v[:, piece:] = terms[:, :qs]
    outs[1].start()
    for i in range(terms.shape[1] // HEAD_DIM - qs // HEAD_DIM):
        at = qs + i * HEAD_DIM
        pair_v[pl.ds(i, piece, stride=2), :] = terms[:, at : at + HEAD_DIM]
    outs[2].start()
    for move in outs:
        move.wait()


def combine_kernel(first, second, wq, wo, spread):
    total = (first[...].astype(F32) + second[...].astype(F32)).astype(BF16)
    for j in range(XS):
        spread[j] = total


def call(kernel, ins, outs, scratch, flops, args, traffic=12 * 2**20):
    return pl.pallas_call(
        kernel,
        out_shape=[out for out, _ in outs],
        in_specs=ins,
        out_specs=[spec for _, spec in outs],
        scratch_shapes=scratch,
        compiler_params=pltpu.CompilerParams(vmem_limit_bytes=24 * 2**20),
        cost_estimate=pl.CostEstimate(flops=flops, bytes_accessed=traffic, transcendentals=2**16),
    )(*args)


def place(section, x, half):
    return (section * XS + x) * HALVES + half


def gather_x(spread):
    return lax.all_to_all(spread, "x", 0, 0)


def hop(block, source, target):
    got = []
    for cross in range(HALVES):
        route = [
            (place(source, x, half), place(target, x, half ^ cross))
            for x in range(XS)
            for half in range(HALVES)
        ]
        got.append(lax.ppermute(block, ("s", "x", "zh"), route))
    return got


def combine(first, second, wq, wo):
    spread = jax.ShapeDtypeStruct((XS,) + first.shape, BF16)
    return call(
        combine_kernel,
        [VMEM] * 2 + [pl.BlockSpec(memory_space=pl.ANY)] * 2,
        [(spread, VMEM)],
        [],
        2**20,
        (first, second, wq, wo),
        2**27,
    )[0]


def nothing(*outs):
    got = pl.pallas_call(
        lambda *refs: None, out_shape=[o for o, _ in outs], out_specs=[HBM for _ in outs]
    )()
    return list(got)


def pair_kernel(here, mine, other, spread):
    width = mine.shape[1]
    first = here[2] == 0
    left = jnp.where(first, mine[...], other[...])
    right = jnp.where(first, other[...], mine[...])
    for j in range(XS):
        spread[j, :, :width] = left
        spread[j, :, width:] = right


def sum_kernel(tokens, sums, block, out):
    total = 0.5 * block[0, :tokens, :].astype(F32)
    for j in range(XS):
        total = total + sums[j].astype(F32)
    out[...] = total.astype(BF16)


def pair_up(start, here):
    route = [
        (place(s, x, half), place(s, x, 1 - half))
        for s in range(SECTIONS)
        for x in range(XS)
        for half in range(HALVES)
    ]
    other = lax.ppermute(start, ("s", "x", "zh"), route)
    spread = jax.ShapeDtypeStruct((XS, start.shape[0], 2 * start.shape[1]), BF16)
    return call(pair_kernel, [SMEM, VMEM, VMEM], [(spread, VMEM)], [], 2**20, (here, start, other))[0]


def shards(hidden_in, lengths, gains, w_query, w_keyval, w_out, grad_out):
    station = lax.axis_index("s")
    rows, length, shard = hidden_in.shape
    tokens = rows * length
    wq = w_query[0]
    width = wq.shape[0]
    wkv = w_keyval[0].reshape(width, -1)
    wo = w_out[0]
    block_width = width // XS
    qs, kvs = wq.shape[1], wkv.shape[1]
    flops = 2 * tokens * width * (2 * qs + kvs)
    tall = qs // HEAD_DIM * length

    here = jnp.stack([station, lax.axis_index("core"), lax.axis_index("zh")])
    start = jnp.where(
        station == 0, hidden_in.reshape(tokens, shard), grad_out.reshape(tokens, shard)
    )
    start = jnp.concatenate([start, jnp.broadcast_to(gains, (16, shard))], 0)
    start_spread = pair_up(start, here)
    start_full, station = lax.optimization_barrier((gather_x(start_spread), station))
    first_block = start_spread
    gain = start_full[:, tokens, :].reshape(1, width)
    first = start_full

    shape = jax.ShapeDtypeStruct
    dma = lambda count: pltpu.SemaphoreType.DMA((count,))
    piece = width // DP
    sent = (shape((XS, tokens, block_width), BF16), VMEM)
    early_pack = (shape((DP, tokens, piece + qs), BF16), HBM)
    late_pack = (shape((XS, tokens + 2 * DP, qs + kvs), BF16), HBM)
    saved = [
        (shape((tokens, 1), F32), VMEM),
        (shape((tokens, qs), BF16), VMEM),
        (shape((tokens, kvs), BF16), VMEM),
        (shape((rows, tall, length), F32), VMEM),
    ]
    over_dp = lambda v: lax.all_to_all(v, ("y", "core"), 0, 0)

    last_section = SECTIONS - 1
    block_out = (shape((tokens, block_width), BF16), HBM)
    factors_out = (shape((DP, tokens, piece + qs), BF16), HBM)
    parts_out = (shape((XS, tokens, block_width), BF16), HBM)

    ready = lambda i: None
    stream = [pltpu.VMEM((width, qs), BF16), pltpu.VMEM((qs, width), BF16), dma(2 * XS)]

    def forward(parts, project, own_copies=False):
        kernel = functools.partial(forward_kernel, rows, length, project, ready)
        if own_copies:
            kernel = functools.partial(streamed, forward_kernel, rows, length, project, False)
        weight = HBM if own_copies else VMEM
        return call(
            kernel,
            [SMEM, VMEM, VMEM, weight, VMEM, weight],
            [sent] * project + [early_pack] + saved,
            [pltpu.VMEM((tokens, width), BF16), pltpu.VMEM((tokens, qs), BF16), dma(2 * DP)]
            + stream * own_copies,
            flops,
            (lengths, parts, gain, wq, wkv, wo),
        )

    def backward(parts_grad, kept, onward):
        kernel = functools.partial(backward_kernel, rows, length, onward, ready)
        if not onward:
            kernel = functools.partial(streamed, backward_kernel, rows, length, onward, True)
        weight = VMEM if onward else HBM
        return call(
            kernel,
            [VMEM] * 7 + [weight, VMEM, weight],
            [sent] * onward + [late_pack],
            [pltpu.VMEM((tokens, qs), BF16), pltpu.VMEM((tokens, kvs), BF16)]
            + [pltpu.VMEM((DP, piece), F32), pltpu.VMEM((2 * DP, piece), BF16), dma(3 * XS)]
            + stream * (not onward),
            flops,
            (parts_grad, kept[0], gain) + tuple(kept[1:]) + (wq, wkv, wo),
        )

    def pass_on(block, sums):
        return call(
            functools.partial(sum_kernel, tokens),
            [VMEM] * 2,
            [(block_out[0], VMEM)],
            [],
            2**20,
            (gather_x(sums), block),
        )[0]

    kept = []
    packed = None
    arrived = None
    for step in range(last_section):

        def work(packed, arrived):
            if arrived is None:
                parts, block = first, first_block
            else:
                spread = combine(*arrived, wq, wo)
                parts, block = gather_x(spread), spread
            got = forward(parts, True, arrived is None)
            return pass_on(block, got[0]), got[1], [parts] * (step > 0) + list(got[2:])

        def rest(packed, arrived):
            empty = nothing(block_out, early_pack, *[parts_out] * (step > 0), *saved)
            return empty[0], empty[1] if packed is None else packed, list(empty[2:])

        block, packed, saved_here = lax.cond(station == step, work, rest, packed, arrived)
        kept.append(saved_here if step else [first] + saved_here)
        arrived = hop(block, step, step + 1)

    def turn(packed, arrived):
        empty, *arrived = lax.optimization_barrier(nothing(factors_out) + list(arrived))
        spread = combine(*arrived, wq, wo)
        parts = gather_x(spread)
        got = forward(parts, False)
        back = backward(first, [parts] + list(got[1:]), True)
        return pass_on(first_block, back[0]), back[1], got[0], empty

    def exchange(packed, arrived):
        empty = nothing(block_out, late_pack, early_pack)
        return tuple(empty) + (over_dp(packed),)

    block, pack, late_factors, early = lax.cond(
        station == last_section, turn, exchange, packed, arrived
    )
    arrived = hop(block, last_section, last_section - 1)

    over_y = lambda v: lax.all_to_all(v, "y", 0, 0)
    swap = lambda v: lax.ppermute(v, "core", [(0, 1), (1, 0)])
    g_kept = first[:, :tokens]
    for step in reversed(range(last_section)):
        onward = step > 0
        if not onward:
            late = lax.cond(
                station == last_section, over_dp, lambda v: nothing(factors_out)[0], late_factors
            )
            late, *arrived = lax.optimization_barrier([late] + list(arrived))

        def work(pack, g_kept, arrived, kept_here):
            spread = combine(*arrived, wq, wo)
            g = gather_x(spread)
            got = backward(g, kept_here, onward)
            if onward:
                return got[1], g, pass_on(spread, got[0])
            return got[0], over_y(g)

        def rest(pack, g_kept, arrived, kept_here):
            return (pack, g_kept, nothing(block_out)[0]) if onward else (pack, over_y(g_kept))

        got = lax.cond(station == step, work, rest, pack, g_kept, arrived, kept[step])
        pack, g_kept = got[:2]
        if onward:
            arrived = hop(got[2], step, step - 1)

    g_own = g_kept
    g_other = swap(g_own)
    own = over_y(pack)
    other = swap(own)
    terms = 0.0
    for item in (own, other):
        item = item[:, tokens:, :piece].astype(F32).reshape(XS, 2, DP, piece)
        terms = terms + jnp.sum(item, (0, 1))
    small = piece // DP
    terms = lax.dynamic_slice_in_dim(terms, lax.axis_index(("y", "core")) * small, small, 1)
    gain_grad = jnp.sum(lax.all_to_all(terms.reshape(DP, 1, small), ("x", "zh"), 0, 0), 0)
    everything = piece + qs + kvs
    scratch = [
        pltpu.VMEM((XS, tokens, piece + qs), BF16),
        pltpu.VMEM((XS * tokens, everything), BF16),
    ]
    total = call(
        functools.partial(weights_kernel, last_section, True),
        [SMEM, HBM, HBM, VMEM, VMEM],
        [(shape((piece, everything), F32), VMEM)],
        scratch + [dma(XS)],
        flops,
        (here, early, late, g_own, own),
    )[0]
    grad_query, grad_pair, grad_out_weight = call(
        functools.partial(weights_kernel, last_section, False),
        [SMEM, HBM, HBM, VMEM, VMEM, VMEM],
        [
            (shape((piece, qs), F32), HBM),
            (shape((piece * kvs // HEAD_DIM, HEAD_DIM), F32), HBM),
            (shape((qs, piece), F32), HBM),
        ],
        scratch
        + [
            pltpu.VMEM((piece, piece + qs), F32),
            pltpu.VMEM((piece * kvs // HEAD_DIM, HEAD_DIM), F32),
            dma(XS),
            dma(3),
        ],
        flops,
        (here, early, late, g_other, other, total),
    )
    return (
        grad_query[None],
        grad_pair.reshape(1, piece, 1, kvs),
        grad_out_weight[None],
        gain_grad[None][:, 0],
    )


def solution(mesh):
    grid = Mesh(mesh.devices.reshape(SECTIONS, XS, HALVES, 4, 2), ("s", "x", "zh", "y", "core"))
    section, tensor, dp = "s", ("x", "zh"), ("y", "core")
    in_specs = (
        P(dp, None, tensor),
        P(dp),
        P(section, tensor),
        P(section, None, tensor),
        P(section, None, tensor, None),
        P(section, tensor, None),
        P(dp, None, tensor),
    )
    out_specs = (
        P(section, dp, tensor),
        P(section, dp, tensor, None),
        P(section, tensor, dp),
        P(section, tensor + dp),
    )
    return jax.shard_map(shards, mesh=grid, in_specs=in_specs, out_specs=out_specs, check_vma=False)
```

```python
import functools

import jax
import jax.numpy as jnp
from jax import lax
from jax.experimental import pallas as pl
from jax.experimental.pallas import tpu as pltpu
from jax.sharding import Mesh, PartitionSpec as P

HEAD_DIM = 128
EPS = 1e-05
NEG = -1e30
F32 = jnp.float32
BF16 = jnp.bfloat16
SECTIONS, XS, HALVES, DP = 4, 4, 2, 8
VMEM = pl.BlockSpec(memory_space=pltpu.VMEM)
SMEM = pl.BlockSpec(memory_space=pltpu.SMEM)
HBM = pl.BlockSpec(memory_space=pltpu.HBM)


def dot(former, latter, dims=((1,), (0,))):
    return lax.dot_general(former, latter, (dims, ((), ())), preferred_element_type=F32)


def copies(pairs, sems):
    at = (lambda i: sems[i]) if isinstance(sems, list) else (lambda i: sems.at[i])
    return [pltpu.make_async_copy(a, b, at(i)) for i, (a, b) in enumerate(pairs)]


def heads_down(wide, row, length):
    part = wide[row * length : (row + 1) * length, :]
    return jnp.concatenate(
        [part[:, a : a + HEAD_DIM] for a in range(0, part.shape[1], HEAD_DIM)], axis=0
    )


def heads_across(tall, length):
    return jnp.concatenate(
        [tall[a : a + length] for a in range(0, tall.shape[0], length)], axis=1
    )


def forward_kernel(rows, length, project, arrive, lens, parts, gain, wq, wkv, wo, *rest):
    if project:
        send, rest = rest[0], rest[1:]
    pack, scale_out, q_out, kv_out, attn_out = rest[:5]
    normed_v, mix_v, out_sems = rest[5:]
    block = parts.shape[2]
    width = XS * block
    piece = width // DP
    tokens = q_out.shape[0]
    outs = []
    for d in range(DP):
        outs.append((normed_v.at[:, pl.ds(d * piece, piece)], pack.at[d, :, pl.ds(0, piece)]))
    for d in range(DP):
        outs.append((mix_v, pack.at[d, :, pl.ds(piece, mix_v.shape[1])]))
    outs = copies(outs, out_sems)
    total = jnp.zeros((tokens, 1), F32)
    for j in range(XS):
        h = parts[j, :tokens, :].astype(F32)
        total = total + jnp.sum(h * h, -1, keepdims=True)
    scale = lax.rsqrt(total / width + EPS)
    scale_out[...] = scale
    q = jnp.zeros(q_out.shape, F32)
    kv = jnp.zeros(kv_out.shape, F32)
    for j in range(XS):
        span = slice(j * block, (j + 1) * block)
        normed = (parts[j, :tokens, :].astype(F32) * scale * gain[:, span].astype(F32)).astype(BF16)
        normed_v[:, span] = normed
        arrive(j)
        q = q + dot(normed, wq[span, :])
        kv = kv + dot(normed, wkv[span, :])
    for move in outs[:DP]:
        move.start()
    q = q.astype(BF16)
    kv = kv.astype(BF16)
    q_out[...] = q
    kv_out[...] = kv
    tall = q.shape[1] // HEAD_DIM * length
    at = lax.broadcasted_iota(jnp.int32, (tall, length), 0) % length
    key_at = lax.broadcasted_iota(jnp.int32, (tall, length), 1)
    mixes = []
    for row in range(rows):
        here = slice(row * length, (row + 1) * length)
        keys, values = kv[here, :HEAD_DIM], kv[here, HEAD_DIM:]
        scores = dot(heads_down(q, row, length), keys, ((1,), (1,))) * HEAD_DIM ** (-0.5)
        scores = jnp.where((key_at <= at) & (key_at < lens[row]), scores, NEG)
        raised = jnp.exp(scores - jnp.max(scores, -1, keepdims=True))
        attn = raised / jnp.sum(raised, -1, keepdims=True)
        attn_out[row] = attn
        mixes.append(heads_across(dot(attn.astype(BF16), values).astype(BF16), length))
    mix = jnp.concatenate(mixes, axis=0)
    mix_v[...] = mix
    for move in outs[DP:]:
        move.start()
    if project:
        for j in range(XS):
            arrive(XS + j)
            send[j] = dot(mix, wo[:, j * block : (j + 1) * block]).astype(BF16)

    for move in outs:
        move.wait()


def backward_kernel(
    rows, length, onward, arrive, grads, parts, gain, scale_in, q_in, kv_in, attn_in,
    wq, wkv, wo, *rest
):
    if onward:
        send, rest = rest[0], rest[1:]
    pack, qg_v, pg_v, gain_v, gain_pair_v, out_sems = rest
    tokens, block = q_in.shape[0], parts.shape[2]
    width = XS * block
    piece = width // DP
    qs, kvs = qg_v.shape[1], pg_v.shape[1]
    outs = []
    for d in range(XS):
        outs.append((qg_v, pack.at[d, pl.ds(0, tokens), pl.ds(0, qs)]))
        outs.append((pg_v, pack.at[d, pl.ds(0, tokens), pl.ds(qs, kvs)]))
    for d in range(XS):
        outs.append((gain_pair_v, pack.at[d, pl.ds(tokens, 2 * DP), pl.ds(0, piece)]))
    outs = copies(outs, out_sems)
    mix_grad = jnp.zeros(q_in.shape, F32)
    for j in range(XS):
        arrive(XS + j)
        mix_grad = mix_grad + dot(grads[j, :tokens, :], wo[:, j * block : (j + 1) * block], ((1,), (1,)))
    mix_grad = mix_grad.astype(BF16)
    q = q_in[...]
    kv = kv_in[...]
    query_grads, pair_grads = [], []
    for row in range(rows):
        here = slice(row * length, (row + 1) * length)
        keys, values = kv[here, :HEAD_DIM], kv[here, HEAD_DIM:]
        attn = attn_in[row]
        mixed = heads_down(mix_grad, row, length)
        value_grad = dot(attn.astype(BF16), mixed, ((0,), (0,)))
        weight_grad = dot(mixed, values, ((1,), (1,)))
        score_grad = attn * (weight_grad - jnp.sum(weight_grad * attn, -1, keepdims=True))
        score_grad = (score_grad * HEAD_DIM ** (-0.5)).astype(BF16)
        query_grads.append(heads_across(dot(score_grad, keys).astype(BF16), length))
        key_grad = dot(score_grad, heads_down(q, row, length), ((0,), (0,)))
        pair_grads.append(jnp.concatenate([key_grad, value_grad], axis=1).astype(BF16))
    query_grad = jnp.concatenate(query_grads, axis=0)
    pair_grad = jnp.concatenate(pair_grads, axis=0)
    qg_v[...] = query_grad
    pg_v[...] = pair_grad

    for move in outs[: 2 * XS]:
        move.start()

    scale = scale_in[...]
    if onward:
        correction = jnp.sum(query_grad.astype(F32) * q.astype(F32), -1, keepdims=True)
        correction += jnp.sum(pair_grad.astype(F32) * kv.astype(F32), -1, keepdims=True)
        pull = scale * scale / width * correction
    for j in range(XS):
        span = slice(j * block, (j + 1) * block)
        arrive(j)
        normed_grad = dot(query_grad, wq[span, :], ((1,), (1,))) + dot(
            pair_grad, wkv[span, :], ((1,), (1,))
        )
        h = parts[j, :tokens, :].astype(F32)
        scaled = normed_grad * scale
        part = jnp.sum(scaled * h, 0, keepdims=True)
        gain_v[2 * j : 2 * j + 1, :] = part[:, :piece]
        gain_v[2 * j + 1 : 2 * j + 2, :] = part[:, piece:]
        if onward:
            send[j] = (scaled * gain[:, span].astype(F32) - h * pull).astype(BF16)
    terms = gain_v[...]
    high = terms.astype(BF16)
    low = (terms - high.astype(F32)).astype(BF16)
    gain_pair_v[...] = jnp.concatenate([high, low], axis=0)

    for move in outs[2 * XS :]:
        move.start()
    for move in outs:
        move.wait()


def streamed(kernel, rows, length, flag, out_first, *refs):
    *refs, wq_v, wo_v, sems = refs
    at = 3 if flag and not out_first else 7
    wq, wo = refs[at], refs[at + 2]
    block = wq.shape[0] // XS
    spans = [pl.ds(j * block, block) for j in range(XS)]
    pairs = [(wq.at[span], wq_v.at[span]) for span in spans]
    pairs += [(wo.at[:, span], wo_v.at[:, span]) for span in spans]
    moves = copies(pairs, sems)
    for move in moves[XS:] + moves[:XS] if out_first else moves:
        move.start()
    refs[at], refs[at + 2] = wq_v, wo_v
    kernel(rows, length, flag, lambda i: moves[i].wait(), *refs)


def weights_kernel(last, own, here, early, late, g, grads, *rest):
    tokens = early.shape[1]
    count, piece = g.shape[0], early.shape[2] // 2
    qs = early.shape[2] - piece
    if own:
        total, factors, wide, sems = rest
    else:
        before, grad_query, grad_pair, grad_out, factors, wide, out_v, pair_v, sems, out_sems = rest
    core = here[1] if own else 1 - here[1]
    load = [
        copies([(source.at[2 * i + core], factors.at[i]) for i in range(count)], sems)
        for source in (early, late)
    ]

    @pl.when(here[0] != last)
    def _():
        for move in load[0]:
            move.start()

    @pl.when(here[0] == last)
    def _():
        for move in load[1]:
            move.start()

    for i in range(count):
        rows = slice(i * tokens, (i + 1) * tokens)
        part = g[i, :tokens, :]
        part = jnp.where(here[1] == 0, part[:, :piece], part[:, piece:])
        wide[rows, :piece] = part
        wide[rows, piece:] = grads[i, :tokens, :]
    for move in load[0]:
        move.wait()
    flat = factors[...].reshape(count * tokens, factors.shape[2])
    if own:
        total[:, :piece] = dot(flat[:, piece:], wide[:, :piece], ((0,), (0,)))
        total[:, piece:] = dot(flat[:, :piece], wide[:, piece:], ((0,), (0,)))
        return
    outs = copies(
        [
            (out_v.at[:, pl.ds(0, piece)], grad_out),
            (out_v.at[:, pl.ds(piece, qs)], grad_query),
            (pair_v, grad_pair),
        ],
        out_sems,
    )
    out_v[:, :piece] = before[:, :piece] + dot(flat[:, piece:], wide[:, :piece], ((0,), (0,)))
    outs[0].start()
    terms = before[:, piece:] + dot(flat[:, :piece], wide[:, piece:], ((0,), (0,)))
    out_v[:, piece:] = terms[:, :qs]
    outs[1].start()
    for i in range(terms.shape[1] // HEAD_DIM - qs // HEAD_DIM):
        at = qs + i * HEAD_DIM
        pair_v[pl.ds(i, piece, stride=2), :] = terms[:, at : at + HEAD_DIM]
    outs[2].start()
    for move in outs:
        move.wait()


def combine_kernel(first, second, wq, wo, spread):
    total = (first[...].astype(F32) + second[...].astype(F32)).astype(BF16)
    for j in range(XS):
        spread[j] = total


def call(kernel, ins, outs, scratch, flops, args, traffic=12 * 2**20):
    return pl.pallas_call(
        kernel,
        out_shape=[out for out, _ in outs],
        in_specs=ins,
        out_specs=[spec for _, spec in outs],
        scratch_shapes=scratch,
        compiler_params=pltpu.CompilerParams(vmem_limit_bytes=24 * 2**20),
        cost_estimate=pl.CostEstimate(flops=flops, bytes_accessed=traffic, transcendentals=2**16),
    )(*args)


def place(section, x, half):
    return (section * XS + x) * HALVES + half


def gather_x(spread):
    return lax.all_to_all(spread, "x", 0, 0)


def hop(block, source, target):
    got = []
    for cross in range(HALVES):
        route = [
            (place(source, x, half), place(target, x, half ^ cross))
            for x in range(XS)
            for half in range(HALVES)
        ]
        got.append(lax.ppermute(block, ("s", "x", "zh"), route))
    return got


def combine(first, second, wq, wo):
    spread = jax.ShapeDtypeStruct((XS,) + first.shape, BF16)
    return call(
        combine_kernel,
        [VMEM] * 2 + [pl.BlockSpec(memory_space=pl.ANY)] * 2,
        [(spread, VMEM)],
        [],
        2**20,
        (first, second, wq, wo),
        2**27,
    )[0]


def nothing(*outs):
    got = pl.pallas_call(
        lambda *refs: None, out_shape=[o for o, _ in outs], out_specs=[HBM for _ in outs]
    )()
    return list(got)


def pair_kernel(here, mine, other, spread):
    width = mine.shape[1]
    first = here[2] == 0
    left = jnp.where(first, mine[...], other[...])
    right = jnp.where(first, other[...], mine[...])
    for j in range(XS):
        spread[j, :, :width] = left
        spread[j, :, width:] = right


def sum_kernel(tokens, sums, block, out):
    total = 0.5 * block[0, :tokens, :].astype(F32)
    for j in range(XS):
        total = total + sums[j].astype(F32)
    out[...] = total.astype(BF16)


def pair_up(start, here):
    route = [
        (place(s, x, half), place(s, x, 1 - half))
        for s in range(SECTIONS)
        for x in range(XS)
        for half in range(HALVES)
    ]
    other = lax.ppermute(start, ("s", "x", "zh"), route)
    spread = jax.ShapeDtypeStruct((XS, start.shape[0], 2 * start.shape[1]), BF16)
    return call(pair_kernel, [SMEM, VMEM, VMEM], [(spread, VMEM)], [], 2**20, (here, start, other))[0]


def shards(hidden_in, lengths, gains, w_query, w_keyval, w_out, grad_out):
    station = lax.axis_index("s")
    rows, length, shard = hidden_in.shape
    tokens = rows * length
    wq = w_query[0]
    width = wq.shape[0]
    wkv = w_keyval[0].reshape(width, -1)
    wo = w_out[0]
    block_width = width // XS
    qs, kvs = wq.shape[1], wkv.shape[1]
    flops = 2 * tokens * width * (2 * qs + kvs)
    tall = qs // HEAD_DIM * length

    here = jnp.stack([station, lax.axis_index("core"), lax.axis_index("zh")])
    start = jnp.where(
        station == 0, hidden_in.reshape(tokens, shard), grad_out.reshape(tokens, shard)
    )
    start = jnp.concatenate([start, jnp.broadcast_to(gains, (16, shard))], 0)
    start_spread = pair_up(start, here)
    start_full, station = lax.optimization_barrier((gather_x(start_spread), station))
    first_block = start_spread
    gain = start_full[:, tokens, :].reshape(1, width)
    first = start_full

    shape = jax.ShapeDtypeStruct
    dma = lambda count: pltpu.SemaphoreType.DMA((count,))
    piece = width // DP
    sent = (shape((XS, tokens, block_width), BF16), VMEM)
    early_pack = (shape((DP, tokens, piece + qs), BF16), HBM)
    late_pack = (shape((XS, tokens + 2 * DP, qs + kvs), BF16), HBM)
    saved = [
        (shape((tokens, 1), F32), VMEM),
        (shape((tokens, qs), BF16), VMEM),
        (shape((tokens, kvs), BF16), VMEM),
        (shape((rows, tall, length), F32), VMEM),
    ]
    over_dp = lambda v: lax.all_to_all(v, ("y", "core"), 0, 0)

    last_section = SECTIONS - 1
    block_out = (shape((tokens, block_width), BF16), HBM)
    factors_out = (shape((DP, tokens, piece + qs), BF16), HBM)
    parts_out = (shape((XS, tokens, block_width), BF16), HBM)

    ready = lambda i: None
    stream = [pltpu.VMEM((width, qs), BF16), pltpu.VMEM((qs, width), BF16), dma(2 * XS)]

    def forward(parts, project, own_copies=False):
        kernel = functools.partial(forward_kernel, rows, length, project, ready)
        if own_copies:
            kernel = functools.partial(streamed, forward_kernel, rows, length, project, False)
        weight = HBM if own_copies else VMEM
        return call(
            kernel,
            [SMEM, VMEM, VMEM, weight, VMEM, weight],
            [sent] * project + [early_pack] + saved,
            [pltpu.VMEM((tokens, width), BF16), pltpu.VMEM((tokens, qs), BF16), dma(2 * DP)]
            + stream * own_copies,
            flops,
            (lengths, parts, gain, wq, wkv, wo),
        )

    def backward(parts_grad, kept, onward):
        kernel = functools.partial(backward_kernel, rows, length, onward, ready)
        if not onward:
            kernel = functools.partial(streamed, backward_kernel, rows, length, onward, True)
        weight = VMEM if onward else HBM
        return call(
            kernel,
            [VMEM] * 7 + [weight, VMEM, weight],
            [sent] * onward + [late_pack],
            [pltpu.VMEM((tokens, qs), BF16), pltpu.VMEM((tokens, kvs), BF16)]
            + [pltpu.VMEM((DP, piece), F32), pltpu.VMEM((2 * DP, piece), BF16), dma(3 * XS)]
            + stream * (not onward),
            flops,
            (parts_grad, kept[0], gain) + tuple(kept[1:]) + (wq, wkv, wo),
        )

    def pass_on(block, sums):
        return call(
            functools.partial(sum_kernel, tokens),
            [VMEM] * 2,
            [(block_out[0], VMEM)],
            [],
            2**20,
            (gather_x(sums), block),
        )[0]

    kept = []
    packed = None
    arrived = None
    for step in range(last_section):

        def work(packed, arrived):
            if arrived is None:
                parts, block = first, first_block
            else:
                spread = combine(*arrived, wq, wo)
                parts, block = gather_x(spread), spread
            got = forward(parts, True, arrived is None)
            return pass_on(block, got[0]), got[1], [parts] * (step > 0) + list(got[2:])

        def rest(packed, arrived):
            empty = nothing(block_out, early_pack, *[parts_out] * (step > 0), *saved)
            return empty[0], empty[1] if packed is None else packed, list(empty[2:])

        block, packed, saved_here = lax.cond(station == step, work, rest, packed, arrived)
        kept.append(saved_here if step else [first] + saved_here)
        arrived = hop(block, step, step + 1)

    def turn(packed, arrived):
        empty, *arrived = lax.optimization_barrier(nothing(factors_out) + list(arrived))
        spread = combine(*arrived, wq, wo)
        parts = gather_x(spread)
        got = forward(parts, False)
        back = backward(first, [parts] + list(got[1:]), True)
        return pass_on(first_block, back[0]), back[1], got[0], empty

    def exchange(packed, arrived):
        empty = nothing(block_out, late_pack, early_pack)
        return tuple(empty) + (over_dp(packed),)

    block, pack, late_factors, early = lax.cond(
        station == last_section, turn, exchange, packed, arrived
    )
    arrived = hop(block, last_section, last_section - 1)

    over_y = lambda v: lax.all_to_all(v, "y", 0, 0)
    swap = lambda v: lax.ppermute(v, "core", [(0, 1), (1, 0)])
    g_kept = first[:, :tokens]
    for step in reversed(range(last_section)):
        onward = step > 0
        if not onward:
            late = lax.cond(
                station == last_section, over_dp, lambda v: nothing(factors_out)[0], late_factors
            )
            late, *arrived = lax.optimization_barrier([late] + list(arrived))

        def work(pack, g_kept, arrived, kept_here):
            spread = combine(*arrived, wq, wo)
            g = gather_x(spread)
            got = backward(g, kept_here, onward)
            if onward:
                return got[1], g, pass_on(spread, got[0])
            return got[0], over_y(g)

        def rest(pack, g_kept, arrived, kept_here):
            return (pack, g_kept, nothing(block_out)[0]) if onward else (pack, over_y(g_kept))

        got = lax.cond(station == step, work, rest, pack, g_kept, arrived, kept[step])
        pack, g_kept = got[:2]
        if onward:
            arrived = hop(got[2], step, step - 1)

    g_own = g_kept
    g_other = swap(g_own)
    own = over_y(pack)
    other = swap(own)
    terms = 0.0
    for item in (own, other):
        item = item[:, tokens:, :piece].astype(F32).reshape(XS, 2, DP, piece)
        terms = terms + jnp.sum(item, (0, 1))
    small = piece // DP
    terms = lax.dynamic_slice_in_dim(terms, lax.axis_index(("y", "core")) * small, small, 1)
    terms, own = lax.optimization_barrier((terms, own))
    gain_grad = jnp.sum(lax.all_to_all(terms.reshape(DP, 1, small), ("x", "zh"), 0, 0), 0)
    everything = piece + qs + kvs
    scratch = [
        pltpu.VMEM((XS, tokens, piece + qs), BF16),
        pltpu.VMEM((XS * tokens, everything), BF16),
    ]
    total = call(
        functools.partial(weights_kernel, last_section, True),
        [SMEM, HBM, HBM, VMEM, VMEM],
        [(shape((piece, everything), F32), VMEM)],
        scratch + [dma(XS)],
        flops,
        (here, early, late, g_own, own),
    )[0]
    grad_query, grad_pair, grad_out_weight = call(
        functools.partial(weights_kernel, last_section, False),
        [SMEM, HBM, HBM, VMEM, VMEM, VMEM],
        [
            (shape((piece, qs), F32), HBM),
            (shape((piece * kvs // HEAD_DIM, HEAD_DIM), F32), HBM),
            (shape((qs, piece), F32), HBM),
        ],
        scratch
        + [
            pltpu.VMEM((piece, piece + qs), F32),
            pltpu.VMEM((piece * kvs // HEAD_DIM, HEAD_DIM), F32),
            dma(XS),
            dma(3),
        ],
        flops,
        (here, early, late, g_other, other, total),
    )
    return (
        grad_query[None],
        grad_pair.reshape(1, piece, 1, kvs),
        grad_out_weight[None],
        gain_grad[None][:, 0],
    )


def solution(mesh):
    grid = Mesh(mesh.devices.reshape(SECTIONS, XS, HALVES, 4, 2), ("s", "x", "zh", "y", "core"))
    section, tensor, dp = "s", ("x", "zh"), ("y", "core")
    in_specs = (
        P(dp, None, tensor),
        P(dp),
        P(section, tensor),
        P(section, None, tensor),
        P(section, None, tensor, None),
        P(section, tensor, None),
        P(dp, None, tensor),
    )
    out_specs = (
        P(section, dp, tensor),
        P(section, dp, tensor, None),
        P(section, tensor, dp),
        P(section, tensor + dp),
    )
    return jax.shard_map(shards, mesh=grid, in_specs=in_specs, out_specs=out_specs, check_vma=False)
```
